256 devices in a mesh: row: 8 (over x, y_hi), col: 32 (over y_lo, z, core).
Axes of the slice: x: 4, y: 4 (y_hi: 2, y_lo: 2; y = y_hi * 2 + y_lo), z: 8, core: 2. Of those that a mesh axis runs over, the one named last changes fastest.
Arguments:
- embed: float32 [65536, 128], P(('row', 'col')), may hold values from -6 to 6
- cotangent: float32 [65536, 128], P(('col', 'row')), may hold values from -6 to 6
- tile_values: float32 [32, 8, 128, 128, 128], P('col', 'row'), may hold values from 0 to 1
- tile_coords: int32 [2, 32, 8, 128], P(None, 'col', 'row'), may hold values from 0 to 63, as said below
- tile_count: int32 [32, 8], P('col', 'row'), may hold values from 1 to 128, as said below
- row_degree: int32 [65536], P(('col', 'row')), may hold values from 16 to 511
- col_degree: int32 [65536], P(('row', 'col')), may hold values from 16 to 511
Outputs:
- propagated: float32 [65536, 128], P(('col', 'row'))
- embed_grad: float32 [65536, 128], P(('row', 'col'))
The draws below stay inside these ranges and needn't reach their ends.
Inputs may be any that keep to these rules, and one draw needn't show every extreme that they name: `tile_coords`: within one device block the slots hold distinct tile positions; the first component is below 16 and the second below 64. `tile_count`: some device block has all 128 slots live.
All inputs are finite; a program needn't handle non-finite values.
Results may differ from the reference program's by a relative error of at most 0.0003.
Values sent between devices are 32-bit elements; how exact they have to be, the bound alone decides.
A program may use at most 128 MiB of HBM per device.

```python
import jax
import jax.numpy as jnp
from jax import lax

D = 128
TILE = 128
NODES_DEV = 256
TILE_CAP = 128
NODES = 65536
N_ROW = 8
N_COL = 32


def draw_tile_coords(key, part):
    row_tiles = NODES_DEV * N_ROW // TILE
    col_tiles = NODES_DEV * N_COL // TILE
    keys = jax.random.split(jax.random.fold_in(key, 11), N_COL * N_ROW)

    def one_block(block_key):
        order = jax.random.permutation(block_key, row_tiles * col_tiles)[:TILE_CAP]
        return jnp.stack([order // col_tiles, order % col_tiles]).astype(jnp.int32)
    blocks = jax.vmap(one_block)(keys)
    return jnp.transpose(blocks, (1, 0, 2)).reshape(2, N_COL, N_ROW, TILE_CAP)


def draw_tile_count(key, part):
    first_key, second_key, third_key, fourth_key = jax.random.split(jax.random.fold_in(key, 23), 4)
    shape = (N_COL, N_ROW)
    light = jax.random.randint(first_key, shape, TILE_CAP // 4, TILE_CAP // 2 + 1)
    hub_flag = jax.random.randint(second_key, shape, 0, 4) == 0
    heavy = TILE_CAP - jax.random.randint(third_key, shape, 0, TILE_CAP // 8 + 1)
    counts = jnp.where(hub_flag, heavy, light).reshape(-1)
    fullest = jax.random.randint(fourth_key, (), 0, N_COL * N_ROW)
    counts = counts.at[fullest].set(TILE_CAP)
    return counts.reshape(shape).astype(jnp.int32)


def place_ends(result, own_key, least, largest):
    longest = result.shape.index(max(result.shape))
    spots = []
    for shift in (0, 1):
        where = [jax.random.randint(jax.random.fold_in(own_key, axis), (), 0, length) for axis, length in enumerate(result.shape)]
        where[longest] = (where[longest] + shift) % result.shape[longest]
        spots.append(tuple(where))
    return result.at[spots[0]].set(least).at[spots[1]].set(largest)


def block_levels(rng, dims, cuts, least, largest):
    factor_of, own = 1.0, jax.random.fold_in(rng, 6)
    for dim, shards_of in cuts:
        draws = jnp.exp(jax.random.uniform(jax.random.fold_in(own, dim), (shards_of,), jnp.float32, least / len(cuts), largest / len(cuts)))
        factor_of = factor_of * jnp.repeat(draws, dims[dim] // shards_of).reshape([-1 if axis == dim else 1 for axis in range(len(dims))])
    return factor_of


def centred(key, extent, deviation, limit, shards=(), kind=jnp.bfloat16):
    result = jax.random.normal(key, extent, jnp.float32) * deviation
    if len(shards) > 0:
        result = block_levels(key, extent, shards, -0.22, 0.18) * result
    return jnp.clip(result, min=-limit, max=limit).astype(kind)


def setup_inputs(seed: int = 0) -> dict:
    seeds = jax.random.split(jax.random.key(seed), 8)
    embed = centred(seeds[0], (NODES, D), 1.0, 6.0, ((0, 256),), jnp.float32)
    cotangent = centred(seeds[1], (NODES, D), 1.0, 6.0, ((0, 256),), jnp.float32)
    tile_values = jnp.clip(1.0 * jax.random.uniform(seeds[2], (N_COL, N_ROW, TILE_CAP, TILE, TILE), jnp.float32) ** block_levels(seeds[2], (N_COL, N_ROW, TILE_CAP, TILE, TILE), ((0, 32), (1, 8)), -0.2, 0.2), 0.0, 1.0)
    tile_coords = draw_tile_coords(jax.random.fold_in(seeds[7], 71), 0)
    tile_count = draw_tile_count(jax.random.fold_in(seeds[7], 71), 0)
    row_degree = place_ends(jax.random.randint(seeds[5], (NODES,), 16, 512), jax.random.fold_in(seeds[5], 1), 16, 511).astype(jnp.int32)
    col_degree = place_ends(jax.random.randint(seeds[6], (NODES,), 16, 512), jax.random.fold_in(seeds[6], 1), 16, 511).astype(jnp.int32)
    return dict(embed=embed, cotangent=cotangent, tile_values=tile_values, tile_coords=tile_coords, tile_count=tile_count, row_degree=row_degree, col_degree=col_degree)


def block_terms(values, rows_at, cols_at, live_count, embed_panel, grad_panel):
    tile_size = values.shape[-1]
    feature_width = embed_panel.shape[1]
    panel_tiles = embed_panel.reshape(-1, tile_size, feature_width)
    grad_tiles = grad_panel.reshape(-1, tile_size, feature_width)
    live_mask = jnp.arange(values.shape[0], dtype=jnp.int32) < live_count
    picked = jnp.take(panel_tiles, cols_at, axis=0)
    forward_each = jnp.einsum('tij,tjd->tid', values, picked, precision=lax.Precision.HIGHEST)
    row_hot = ((rows_at[None, :] == jnp.arange(grad_tiles.shape[0], dtype=jnp.int32)[:, None]) & live_mask[None, :]).astype(values.dtype)
    forward = jnp.einsum('at,tid->aid', row_hot, forward_each, precision=lax.Precision.HIGHEST)
    grad_picked = jnp.take(grad_tiles, rows_at, axis=0)
    backward_each = jnp.einsum('tij,tid->tjd', values, grad_picked, precision=lax.Precision.HIGHEST)
    col_hot = ((cols_at[None, :] == jnp.arange(panel_tiles.shape[0], dtype=jnp.int32)[:, None]) & live_mask[None, :]).astype(values.dtype)
    backward = jnp.einsum('bt,tjd->bjd', col_hot, backward_each, precision=lax.Precision.HIGHEST)
    return (forward.reshape(-1, feature_width), backward.reshape(-1, feature_width))

def reference(embed, cotangent, tile_values, tile_coords, tile_count, row_degree, col_degree):
    rows_block = NODES // N_COL
    cols_block = NODES // N_ROW
    scaled = embed * lax.rsqrt(col_degree.astype(jnp.float32))[:, None]
    grad_scaled = cotangent * lax.rsqrt(row_degree.astype(jnp.float32))[:, None]

    def outer(grad_total, block_col):
        grad_panel = lax.dynamic_slice_in_dim(grad_scaled, block_col * rows_block, rows_block, 0)

        def inner(carry, block_row):
            forward_total, grad_inner = carry
            embed_panel = lax.dynamic_slice_in_dim(scaled, block_row * cols_block, cols_block, 0)
            forward, backward = block_terms(tile_values[block_col, block_row], tile_coords[0, block_col, block_row], tile_coords[1, block_col, block_row], tile_count[block_col, block_row], embed_panel, grad_panel)
            first_row = (block_row * cols_block).astype(jnp.int32)
            current = lax.dynamic_slice_in_dim(grad_inner, first_row, cols_block, 0)
            grad_inner = lax.dynamic_update_slice_in_dim(grad_inner, current + backward, first_row, 0)
            return ((forward_total + forward, grad_inner), None)
        start_forward = jnp.zeros((rows_block, embed.shape[1]), embed.dtype)
        (forward_total, grad_total), unused = lax.scan(inner, (start_forward, grad_total), jnp.arange(N_ROW, dtype=jnp.int32))
        return (grad_total, forward_total)
    grad_total, forward_blocks = lax.scan(outer, jnp.zeros_like(embed), jnp.arange(N_COL, dtype=jnp.int32))
    propagated = forward_blocks.reshape(NODES, embed.shape[1]) * lax.rsqrt(row_degree.astype(jnp.float32))[:, None]
    embed_grad = grad_total * lax.rsqrt(col_degree.astype(jnp.float32))[:, None]
    return (propagated, embed_grad)
```

```python
import jax
import jax.numpy as jnp
from jax import lax
from jax.experimental import pallas as pl
from jax.experimental.pallas import tpu as pltpu
from jax.sharding import PartitionSpec as P

MESH = pl.DeviceIdType.MESH
F32 = jnp.float32
BF16 = jnp.bfloat16
T = 128
SLOTS = 128
NX, NZ = 4, 8
N_COPIES = 156


class Comm:
    def __init__(self, send_sems, recv_sems):
        self.send_sems, self.recv_sems, self.n, self.all = send_sems, recv_sems, 0, []

    def send(self, src, dst, dev, land=None):
        copy = pltpu.make_async_remote_copy(
            src_ref=src,
            dst_ref=dst,
            send_sem=self.send_sems.at[self.n],
            recv_sem=self.recv_sems.at[self.n],
            device_id=dev,
            device_id_type=MESH,
        )
        copy.start()
        back = pltpu.make_async_remote_copy(
            src_ref=src,
            dst_ref=dst if land is None else land,
            send_sem=self.send_sems.at[self.n],
            recv_sem=self.recv_sems.at[self.n],
            device_id=dev,
            device_id_type=MESH,
        )
        self.n += 1
        self.all.append(copy)
        return back.wait_recv

    def drain(self):
        for copy in self.all:
            copy.wait_send()


def split(value):
    high = value.astype(BF16)
    return high, (value - high.astype(F32)).astype(BF16)


def kernel(
    idx, embed, cot, rdeg, cdeg, values,
    prop_out, grad_out,
    panel, pairs, vraw, vpair, fwd_each, bwd_each, part, from_core, ring, from_y,
    gpanel, gpair, fpart, xring, relay, frelay, from_yh,
    send_sems, recv_sems, load_sems,
):
    row, col = lax.axis_index("row"), lax.axis_index("col")
    x, yh = lax.div(row, 2), lax.rem(row, 2)
    core, chip = lax.rem(col, 2), lax.div(col, 2)
    yl, z = lax.div(chip, NZ), lax.rem(chip, NZ)
    turn = 1 - 2 * core

    def zat(d):
        return lax.rem(z + turn * d + NZ, NZ)

    def xat(d):
        return lax.rem(x + turn * d + NX, NX)

    def colof(y, zz, c):
        return (y * NZ + zz) * 2 + c

    def ctile(other, d, h, c=None, sign=1):
        y = 1 - yl if other else yl
        return colof(y, zat(sign * d), core if c is None else c) * 2 + h

    def rtile(other, d, h):
        return (xat(d) * 2 + (1 - yh if other else yh)) * 2 + h

    partner = (row, col + turn)
    za = (row, colof(yl, zat(1), core))
    zb = (row, colof(yl, zat(-1), core))
    ypair = (row, colof(1 - yl, z, core))
    cross = (x * 2 + 1 - yh, colof(1 - yl, z, core))
    xa = (xat(1) * 2 + yh, col)
    xb = (xat(-1) * 2 + yh, col)
    first_pair = 1 - core
    hop1 = (x * 2 + (yh * first_pair + (1 - yh) * core), colof(1 - yl, z, core))
    hop2 = (x * 2 + (yh * core + (1 - yh) * first_pair), colof(1 - yl, z, core))
    relay_yh = yh * first_pair + (1 - yh) * core

    loads = []
    group = SLOTS // 8
    for g in range(8):
        piece = pl.ds(g * group, group)
        load = pltpu.make_async_copy(values.at[piece], vraw.at[piece], load_sems.at[g])
        load.start()
        loads.append(load)

    for h in range(2):
        half = pl.ds(h * T, T)
        rs = lax.rsqrt(rdeg[pl.ds(h, 1), :].astype(F32))
        cs = lax.rsqrt(cdeg[pl.ds(h, 1), :].astype(F32))
        gpanel[rtile(0, 0, h)] = cot[half, :].T * rs
        panel[ctile(0, 0, h)] = (embed[half, :].T * cs).T
    fwd_each[SLOTS] = jnp.zeros((T, T), F32)
    bwd_each[SLOTS] = jnp.zeros((T, T), F32)

    barrier = pltpu.get_barrier_semaphore()
    for dev in (partner, za, zb, ypair, cross, xa, xb):
        pl.semaphore_signal(barrier, inc=1, device_id=dev, device_id_type=MESH)
    pl.semaphore_wait(barrier, 7)

    comm = Comm(send_sems, recv_sems)

    def share(ref, tile, dev, land):
        return comm.send(ref.at[tile], ref.at[tile], dev, ref.at[land])

    to_core = []

    def col_core(tile, land):
        to_core.append(share(panel, tile, partner, land))

    def key_land(other, d, h):
        return ctile(other, d, h, 1 - core, -1)

    relayed = [
        comm.send(gpanel.at[rtile(0, 0, h)], relay.at[h], hop1) for h in range(2)
    ]
    xa1, xb1 = {}, {}
    for h in range(2):
        xa1[0, h] = share(gpanel, rtile(0, 0, h), xa, rtile(0, -1, h))
        xb1[0, h] = share(gpanel, rtile(0, 0, h), xb, rtile(0, 1, h))
    y_first = share(panel, ctile(0, 0, 0), ypair, ctile(1, 0, 0))
    za_got, zb_got, y_got = {}, {}, {}

    def z_send(p, k):
        other, h = ((0, 0), (0, 1), (1, 0))[p]
        if k < 4:
            za_got[k + 1, p] = share(panel, ctile(other, -k, h), za, ctile(other, -k - 1, h))
        if k < 3:
            zb_got[k + 1, p] = share(panel, ctile(other, k, h), zb, ctile(other, k + 1, h))

    z_send(0, 0)
    z_send(1, 0)
    y_got[0] = share(panel, ctile(0, 0, 1), ypair, ctile(1, 0, 1))
    for h in range(2):
        col_core(ctile(0, 0, h), key_land(0, 0, h))

    def ev_relay():
        for h in range(2):
            relayed[h]()
        for h in range(2):
            tile = (x * 2 + relay_yh) * 2 + h
            relayed[h] = comm.send(
                relay.at[h], gpanel.at[tile], hop2, gpanel.at[rtile(1, 0, h)]
            )

    def ev_y_first():
        y_first()
        z_send(2, 0)
        col_core(ctile(1, 0, 0), key_land(1, 0, 0))

    def ev_z(k, p):
        def run():
            other, h = ((0, 0), (0, 1), (1, 0))[p]
            za_got[k, p]()
            if k < 4:
                zb_got[k, p]()
            if k < 4:
                z_send(p, k)
            signs = (-1, 1) if k < 4 else (-1,)
            for s in signs:
                tile = ctile(other, s * k, h)
                if p == 1:
                    y_got[s * k] = share(panel, tile, ypair, ctile(1, s * k, 1))
                col_core(tile, key_land(other, s * k, h))

        return run

    def ev_y(d):
        def run():
            y_got[d]()
            col_core(ctile(1, d, 1), key_land(1, d, 1))

        return run

    def ev_x_other():
        for h in range(2):
            relayed[h]()
            xa1[1, h] = share(gpanel, rtile(1, 0, h), xa, rtile(1, -1, h))
            xb1[1, h] = share(gpanel, rtile(1, 0, h), xb, rtile(1, 1, h))

    xa2 = {}

    def ev_x(other):
        def run():
            for h in range(2):
                xa1[other, h]()
                xa2[other, h] = share(gpanel, rtile(other, -1, h), xa, rtile(other, -2, h))
                xb1[other, h]()

        return run

    def ev_x_end():
        for key in ((0, 0), (0, 1), (1, 0), (1, 1)):
            xa2[key]()

    def ev_core_end():
        for wait in to_core:
            wait()

    def do_split(g):
        def run():
            loads[g].wait()

            def body(i, carry):
                for u in range(2):
                    t = g * group + i * 2 + u
                    high, low = split(vraw[t])
                    vpair[t, pl.ds(0, T), :] = high
                    vpair[t, pl.ds(T, T), :] = low
                return carry

            lax.fori_loop(0, group // 2, body, 0)

        return run

    def do_gsplit():
        def body(r, carry):
            high, low = split(gpanel[r])
            gpair[r, pl.ds(0, T), :] = high
            gpair[r, pl.ds(T, T), :] = low
            return carry

        lax.fori_loop(0, 4 * NX, body, 0)

    def do_bwd(g):
        def run():
            def body(i, carry):
                for u in range(4):
                    t = g * group + i * 4 + u
                    g2 = gpair[idx[0, t]]
                    out = jnp.dot(
                        jnp.concatenate([g2, g2], axis=1), vpair[t], preferred_element_type=F32
                    )
                    bwd_each[t] = out[:T] + out[T:] + bwd_each[idx[3, t]]
                return carry

            lax.fori_loop(0, group // 4, body, 0)

        return run

    def do_ssplit():
        def body(c, carry):
            high, low = split(panel[c])
            pairs[c, :, pl.ds(0, T)] = high
            pairs[c, :, pl.ds(T, T)] = low
            return carry

        lax.fori_loop(0, 8 * NZ, body, 0)

    def do_fwd(g):
        def run():
            def body(i, carry):
                for u in range(4):
                    t = g * group + i * 4 + u
                    s2 = pairs[idx[1, t]]
                    v2 = jnp.concatenate([vpair[t, pl.ds(0, T), :], vpair[t, pl.ds(T, T), :]], axis=1)
                    out = jnp.dot(
                        v2, jnp.concatenate([s2, s2], axis=0), preferred_element_type=F32
                    )
                    fwd_each[t] = out[:, :T] + out[:, T:] + fwd_each[idx[2, t]]
                return carry

            lax.fori_loop(0, group // 4, body, 0)

        return run

    plan = [
        ev_y_first, do_split(0),
        ev_relay, do_split(1),
        ev_z(1, 0), do_split(2), ev_z(1, 1), do_split(3),
        ev_x(0), do_split(4), ev_x_other, do_split(5), ev_z(1, 2), ev_y(0), do_split(6),
        ev_z(2, 0), do_split(7), ev_z(2, 1), ev_y(-1), ev_y(1),
        ev_x(1), ev_z(2, 2), ev_x_end, do_gsplit,
        do_bwd(0), ev_z(3, 0), do_bwd(1), ev_z(3, 1), do_bwd(2), ev_y(-2), ev_y(2),
        do_bwd(3), ev_z(3, 2), do_bwd(4), ev_z(4, 0), do_bwd(5), ev_z(4, 1), ev_y(-3), ev_y(3),
        do_bwd(6), ev_z(4, 2), ev_y(-4), do_bwd(7),
    ]
    for step in plan:
        step()

    def pick(tile, each, last):
        part[tile] = each[last]

    order = (-4, 4)
    need = [(other, d, h) for d in (4, 3, -3, 2, -2, 1, -1, 0) for other, h in ((0, 0), (1, 0), (1, 1), (0, 1))]
    core_got = {}
    for n, (other, d, h) in enumerate(need):
        tile = ctile(other, d, h, 1 - core, -1)
        part[tile] = bwd_each[idx[5, tile]]
        core_got[other, d, h] = comm.send(part.at[tile], from_core.at[n], partner)
    where = {key: n for n, key in enumerate(need)}
    own_y, a_got, b_got = {}, {}, {}

    def ring_send(p, d, sign, slot, got):
        other, h = ((0, 0), (1, 0), (0, 1))[p]
        got[p, slot] = comm.send(
            part.at[ctile(other, d, h)], ring.at[slot * 3 + p], za if sign > 0 else zb
        )

    def merge(other, d, h):
        tile = ctile(other, d, h)
        core_got[other, d, h]()
        part[tile] = bwd_each[idx[5, tile]] + from_core[where[other, d, h]]

    def ev_merge(d):
        def run():
            for other, h in ((0, 0), (1, 0), (1, 1), (0, 1)):
                merge(other, d, h)
                if (other, h) == (1, 1):
                    own_y[d] = comm.send(part.at[ctile(1, d, 1)], from_y.at[d % NZ], ypair)
                if d == 4 and h == 0:
                    ring_send(other, 4, 1, 3, a_got)
                if d == -3 and h == 0:
                    ring_send(other, -3, -1, 6, b_got)

        return run

    def ev_merge_y(d):
        def run():
            own_y[d]()
            part[ctile(0, d, 1)] += from_y[d % NZ]
            if d == 4:
                ring_send(2, 4, 1, 3, a_got)
            if d == -3:
                ring_send(2, -3, -1, 6, b_got)

        return run

    def ev_a(p, left):
        def run():
            other, h = ((0, 0), (1, 0), (0, 1))[p]
            a_got[p, left]()
            part[ctile(other, left, h)] += ring[left * 3 + p]
            if left:
                ring_send(p, left, 1, left - 1, a_got)

        return run

    def ev_b(p, left):
        def run():
            other, h = ((0, 0), (1, 0), (0, 1))[p]
            b_got[p, 4 + left]()
            part[ctile(other, -left, h)] += ring[(4 + left) * 3 + p]
            if left:
                ring_send(p, -left, -1, 4 + left - 1, b_got)

        return run

    def ev_grad_y():
        own_y["end"] = comm.send(part.at[ctile(1, 0, 0)], from_y.at[NZ], ypair)

    def ev_grad_end():
        own_y["end"]()
        for h in range(2):
            total = part[ctile(0, 0, h)]
            if h == 0:
                total = total + from_y[NZ]
            cs = lax.rsqrt(cdeg[pl.ds(h, 1), :].astype(F32))
            grad_out[pl.ds(h * T, T), :] = (total * cs).T

    fa, fb = {}, {}

    def ev_f_start():
        for r in range(4 * NX):
            fpart[r] = fwd_each[idx[4, r]]
        for other in (1, 0):
            for h in range(2):
                fa[other, h] = comm.send(fpart.at[rtile(other, 2, h)], xring.at[other * 2 + h], xa)
                fb[other, h] = comm.send(fpart.at[rtile(other, -1, h)], xring.at[4 + other * 2 + h], xb)

    def ev_f_mid(other):
        def run():
            for h in range(2):
                fa[other, h]()
                fpart[rtile(other, 1, h)] += xring[other * 2 + h]
                fa[other, h] = comm.send(
                    fpart.at[rtile(other, 1, h)], xring.at[8 + other * 2 + h], xa
                )

        return run

    def ev_f_last(other):
        def run():
            for h in range(2):
                fa[other, h]()
                fb[other, h]()
                fpart[rtile(other, 0, h)] += xring[4 + other * 2 + h] + xring[8 + other * 2 + h]
                if other:
                    relayed[h] = comm.send(fpart.at[rtile(1, 0, h)], frelay.at[h], hop1)

        return run

    def ev_f_relay():
        for h in range(2):
            relayed[h]()
            relayed[h] = comm.send(frelay.at[h], from_yh.at[h], hop2)

    def ev_f_end():
        for h in range(2):
            relayed[h]()
            rs = lax.rsqrt(rdeg[pl.ds(h, 1), :].astype(F32))
            total = fpart[rtile(0, 0, h)] + from_yh[h]
            prop_out[pl.ds(h * T, T), :] = (total.T * rs).T

    plan = [
        ev_merge(4), ev_merge(3), ev_merge(-3), ev_merge_y(4), ev_merge_y(3), ev_merge_y(-3),
        ev_merge(2), ev_merge(-2), ev_merge_y(2), ev_merge_y(-2),
        ev_core_end, do_ssplit,
        ev_a(0, 3), ev_b(0, 2), ev_a(1, 3), ev_b(1, 2),
        ev_merge(1), ev_merge(-1), ev_merge_y(1), ev_merge_y(-1), ev_merge(0), ev_merge_y(0),
        do_fwd(0), ev_a(2, 3), ev_b(2, 2),
        do_fwd(1), ev_a(0, 2), ev_b(0, 1), do_fwd(2), ev_a(1, 2), ev_b(1, 1),
        do_fwd(3), ev_a(2, 2), ev_b(2, 1), do_fwd(4), do_fwd(5), ev_a(0, 1), ev_b(0, 0),
        do_fwd(6), ev_a(1, 1), ev_b(1, 0), do_fwd(7), ev_f_start,
        ev_a(2, 1), ev_b(2, 0), ev_f_mid(1), ev_f_mid(0), ev_a(1, 0), ev_grad_y, ev_a(0, 0),
        ev_f_last(1), ev_a(2, 0), ev_f_relay, ev_f_last(0), ev_grad_end, ev_f_end,
    ]
    for step in plan:
        step()
    comm.drain()


def tables(coords, count):
    rows, cols = coords[0, 0, 0], coords[1, 0, 0]
    slot = jnp.arange(SLOTS, dtype=jnp.int32)
    live = slot < count[0, 0]

    def latest(asked, below, keys):
        hit = (asked[:, None] == keys[None, :]) & live[None, :] & (slot[None, :] < below[:, None])
        best = jnp.max(jnp.where(hit, slot[None, :], -1), axis=1)
        return jnp.where(best < 0, SLOTS, best)

    full = jnp.full((SLOTS,), SLOTS, jnp.int32)
    return jnp.stack([
        rows, cols,
        latest(rows, slot, rows), latest(cols, slot, cols),
        latest(slot, full, rows), latest(slot, full, cols),
    ])


def per_device(embed, cotangent, tile_values, tile_coords, tile_count, row_degree, col_degree):
    vmem = pl.BlockSpec(memory_space=pltpu.VMEM)
    tile = lambda n, dtype=F32, a=T, b=T: pltpu.VMEM((n, a, b), dtype)
    return pl.pallas_call(
        kernel,
        out_shape=(jax.ShapeDtypeStruct((2 * T, T), F32), jax.ShapeDtypeStruct((2 * T, T), F32)),
        in_specs=[pl.BlockSpec(memory_space=pltpu.SMEM), vmem, vmem, vmem, vmem, pl.BlockSpec(memory_space=pl.ANY)],
        out_specs=(vmem, vmem),
        scratch_shapes=[
            tile(64), tile(64, BF16, T, 2 * T), tile(SLOTS), tile(SLOTS, BF16, 2 * T, T),
            tile(SLOTS + 1), tile(SLOTS + 1), tile(64), tile(32), tile(21), tile(9),
            tile(16), tile(16, BF16, 2 * T, T), tile(16), tile(12), tile(2), tile(2), tile(2),
            pltpu.SemaphoreType.DMA((N_COPIES,)),
            pltpu.SemaphoreType.DMA((N_COPIES,)),
            pltpu.SemaphoreType.DMA((8,)),
        ],
        compiler_params=pltpu.CompilerParams(
            collective_id=0, has_side_effects=True, vmem_limit_bytes=62 * 1024 * 1024
        ),
    )(
        tables(tile_coords, tile_count), embed, cotangent,
        row_degree.reshape(2, T), col_degree.reshape(2, T), tile_values[0, 0],
    )


def solution(mesh):
    return jax.shard_map(
        per_device,
        mesh=mesh,
        in_specs=(
            P(("row", "col"), None),
            P(("col", "row"), None),
            P("col", "row", None, None, None),
            P(None, "col", "row", None),
            P("col", "row"),
            P(("col", "row")),
            P(("row", "col")),
        ),
        out_specs=(P(("col", "row"), None), P(("row", "col"), None)),
        check_vma=False,
    )
```

```python
import jax
import jax.numpy as jnp
from jax import lax
from jax.experimental import pallas as pl
from jax.experimental.pallas import tpu as pltpu
from jax.sharding import PartitionSpec as P

MESH = pl.DeviceIdType.MESH
F32 = jnp.float32
BF16 = jnp.bfloat16
T = 128
SLOTS = 128
NX, NZ = 4, 8
UNROLL = 16
VMEM_LIMIT = 58 * 1024 * 1024
N_RECV = 83
N_AG = N_RS = 76


class Comm:
    def __init__(self, send_sem, recv_sems):
        self.send_sem, self.recv_sems, self.n, self.tiles = send_sem, recv_sems, 0, [0, 0]
        self.phase = 0

    def slot(self):
        self.n += 1
        return self.n - 1

    def copy(self, src, dst, dev, slot):
        return pltpu.make_async_remote_copy(
            src_ref=src,
            dst_ref=dst,
            send_sem=self.send_sem.at[self.phase],
            recv_sem=self.recv_sems.at[slot],
            device_id=dev,
            device_id_type=MESH,
        )

    def send(self, src, dst, dev, land=None, slot=None, n=1):
        slot = self.slot() if slot is None else slot
        self.copy(src, dst, dev, slot).start()
        self.tiles[self.phase] += n
        return lambda: self.copy(src, dst if land is None else land, dev, slot).wait_recv()


def split(value):
    high = value.astype(BF16)
    return high, (value - high.astype(F32)).astype(BF16)


def kernel(
    embed_hbm, cot_hbm, rdeg_hbm, cdeg_hbm, coords_hbm, count_hbm, values,
    out,
    embed, cot, rdeg, cdeg, coords, count, table, idx,
    panel, pairs, vraw, vpair, fwd_each, bwd_each, part, from_core, ring, from_y,
    gpanel, gpair, fpart, xring, from_yh,
    send_sem, recv_sems, load_sems,
):
    row, col = lax.axis_index("row"), lax.axis_index("col")
    x, yh = lax.div(row, 2), lax.rem(row, 2)
    core, chip = lax.rem(col, 2), lax.div(col, 2)
    yl, z = lax.div(chip, NZ), lax.rem(chip, NZ)
    turn = 1 - 2 * core

    def zat(d):
        return lax.rem(z + turn * d + NZ, NZ)

    def xat(d):
        return lax.rem(x + turn * d + NX, NX)

    def colof(y, zz, c):
        return (y * NZ + zz) * 2 + c

    def ctile(other, d, h, c=None, sign=1):
        y = 1 - yl if other else yl
        return colof(y, zat(sign * d), core if c is None else c) * 2 + h

    def rtile(other, d, h):
        return (xat(d) * 2 + (1 - yh if other else yh)) * 2 + h

    partner = (row, col + turn)
    za = (row, colof(yl, zat(1), core))
    zb = (row, colof(yl, zat(-1), core))
    ypair = (row, colof(1 - yl, z, core))
    ypeer = (x * 2 + 1 - yh, col)
    xa = (xat(1) * 2 + yh, col)
    xb = (xat(-1) * 2 + yh, col)

    barrier = pltpu.get_barrier_semaphore()
    for dev in (za, zb, xa, xb, ypair, ypeer, partner):
        pl.semaphore_signal(barrier, inc=1, device_id=dev, device_id_type=MESH)

    inputs = []
    for n, (src, dst) in enumerate((
        (cot_hbm, cot), (rdeg_hbm, rdeg), (embed_hbm, embed), (cdeg_hbm, cdeg), (coords_hbm, coords), (count_hbm, count)
    )):
        load = pltpu.make_async_copy(src, dst, load_sems.at[n])
        load.start()
        inputs.append(load)
    loads = []
    group = SLOTS // 8
    for g in range(4):
        piece = pl.ds(g * 2 * group, 2 * group)
        load = pltpu.make_async_copy(values.at[piece], vraw.at[piece], load_sems.at[6 + g])
        load.start()
        loads.append(load)
    for load in inputs:
        load.wait()

    for h in range(2):
        half = pl.ds(h * T, T)
        rs = lax.rsqrt(rdeg[pl.ds(h, 1), :].astype(F32))
        cs = lax.rsqrt(cdeg[pl.ds(h, 1), :].astype(F32))
        gpanel[rtile(0, 0, h)] = cot[half, :].T * rs
        panel[ctile(0, 0, h)] = (embed[half, :].T * cs).T
    pl.semaphore_wait(barrier, 7)

    comm = Comm(send_sem, recv_sems)

    def share(ref, tile, dev, land, n=1, slot=None):
        if n > 1:
            return comm.send(ref.at[pl.ds(tile, n)], ref.at[pl.ds(tile, n)], dev, ref.at[pl.ds(land, n)], slot, n)
        return comm.send(ref.at[tile], ref.at[tile], dev, ref.at[land], slot)

    core_slot = comm.slot()

    def col_core(tile):
        comm.send(panel.at[tile], panel.at[tile], partner, slot=core_slot)

    got_yh = share(gpanel, rtile(0, 0, 0), ypeer, rtile(1, 0, 0), 2)
    xa1, xb1, xa2 = {}, {}, {}
    xa1[0] = share(gpanel, rtile(0, 0, 0), xa, rtile(0, -1, 0), 2)
    xb1[0] = share(gpanel, rtile(0, 0, 0), xb, rtile(0, 1, 0), 2)
    za_got, zb_got, y_got = {}, {}, {}
    PIECES = ((0, 0), (0, 1), (1, 0))

    def z_send(p, k):
        other, h = PIECES[p]
        if k < 4:
            za_got[k + 1, p] = share(panel, ctile(other, -k, h), za, ctile(other, -k - 1, h))
        if k < 3:
            zb_got[k + 1, p] = share(panel, ctile(other, k, h), zb, ctile(other, k + 1, h))

    z_send(0, 0)
    y_first = share(panel, ctile(0, 0, 0), ypair, ctile(1, 0, 0))
    z_send(1, 0)
    y_got[0] = share(panel, ctile(0, 0, 1), ypair, ctile(1, 0, 1))
    for h in range(2):
        col_core(ctile(0, 0, h))

    sub = lax.broadcasted_iota(jnp.int32, (T, T), 0)
    lane = lax.broadcasted_iota(jnp.int32, (T, T), 1)
    live = sub < count[0, 0]

    def latest(hit):
        best = jnp.max(jnp.where(hit & live, sub, -1), axis=0, keepdims=True)
        return jnp.where(best < 0, SLOTS, best)

    for n in range(2):
        key = jnp.broadcast_to(coords[pl.ds(n, 1), :], (T, T))
        down = key.T
        table[pl.ds(n, 1), :] = coords[pl.ds(n, 1), :]
        table[pl.ds(2 + n, 1), :] = latest((down == key) & (sub < lane))
        table[pl.ds(4 + n, 1), :] = latest(down == lane)
    to_smem = pltpu.make_async_copy(table, idx, load_sems.at[10])
    to_smem.start()
    fwd_each[SLOTS] = jnp.zeros((T, T), F32)
    bwd_each[SLOTS] = jnp.zeros((T, T), F32)

    def ev_row_y():
        got_yh()
        xa1[1] = share(gpanel, rtile(1, 0, 0), xa, rtile(1, -1, 0), 2)
        xb1[1] = share(gpanel, rtile(1, 0, 0), xb, rtile(1, 1, 0), 2)

    def ev_x(other):
        def run():
            xa1[other]()
            xa2[other] = share(gpanel, rtile(other, -1, 0), xa, rtile(other, -2, 0), 2)
            xb1[other]()

        return run

    def ev_x_end():
        xa2[0]()
        xa2[1]()

    def ev_y_first():
        y_first()
        z_send(2, 0)
        col_core(ctile(1, 0, 0))

    def ev_z(k, p):
        def run():
            other, h = PIECES[p]
            za_got[k, p]()
            if k < 4:
                zb_got[k, p]()
                z_send(p, k)
            for s in (-1, 1) if k < 4 else (-1,):
                tile = ctile(other, s * k, h)
                if p == 1:
                    y_got[s * k] = share(panel, tile, ypair, ctile(1, s * k, 1))
                col_core(tile)

        return run

    def ev_y(d):
        def run():
            y_got[d]()
            col_core(ctile(1, d, 1))

        return run

    def ev_core_end():
        comm.copy(panel.at[pl.ds(0, 32)], panel.at[pl.ds(0, 32)], partner, core_slot).wait_recv()

    def do_split(g):
        def run():
            if g % 2 == 0:
                loads[g // 2].wait()

            def body(i, carry):
                for u in range(2):
                    t = g * group + i * 2 + u
                    high, low = split(vraw[t])
                    vpair[t, pl.ds(0, T), :] = high
                    vpair[t, pl.ds(T, T), :] = low
                return carry

            lax.fori_loop(0, group // 2, body, 0)

        return run

    def do_gsplit():
        to_smem.wait()

        def body(r, carry):
            high, low = split(gpanel[r])
            gpair[r, pl.ds(0, T), :] = high
            gpair[r, pl.ds(T, T), :] = low
            return carry

        lax.fori_loop(0, 4 * NX, body, 0)

    def do_bwd(g):
        def run():
            def body(i, carry):
                for u in range(UNROLL):
                    t = g * group + i * UNROLL + u
                    g2 = gpair[idx[0, t]]
                    res = jnp.dot(
                        jnp.concatenate([g2, g2], axis=1), vpair[t], preferred_element_type=F32
                    )
                    bwd_each[t] = res[:T] + res[T:] + bwd_each[idx[3, t]]
                return carry

            lax.fori_loop(0, group // UNROLL, body, 0)

        return run

    def do_ssplit():
        def body(c, carry):
            for u in range(2):
                high, low = split(panel[c * 2 + u])
                pairs[c * 2 + u, :, pl.ds(0, T)] = high
                pairs[c * 2 + u, :, pl.ds(T, T)] = low
            return carry

        lax.fori_loop(0, 4 * NZ, body, 0)

    def do_fwd(g):
        def run():
            def body(i, carry):
                for u in range(UNROLL):
                    t = g * group + i * UNROLL + u
                    s2 = pairs[idx[1, t]]
                    v2 = jnp.concatenate([vpair[t, pl.ds(0, T), :], vpair[t, pl.ds(T, T), :]], axis=1)
                    res = jnp.dot(
                        v2, jnp.concatenate([s2, s2], axis=0), preferred_element_type=F32
                    )
                    fwd_each[t] = res[:, :T] + res[:, T:] + fwd_each[idx[2, t]]
                return carry

            lax.fori_loop(0, group // UNROLL, body, 0)

        return run

    plan = [
        do_split(0), do_split(1), do_split(2), do_split(3), ev_z(1, 0),
        do_split(4), do_split(5), ev_x(0), ev_row_y, ev_z(1, 1), ev_y_first, do_split(6), do_split(7),
        ev_y(0), ev_z(2, 0), ev_z(2, 1), ev_y(-1), ev_y(1), ev_z(1, 2), ev_x(1),
        ev_z(3, 0), ev_z(3, 1), ev_z(2, 2), ev_x_end, do_gsplit,
        do_bwd(0), ev_y(-2), ev_y(2), do_bwd(1), ev_z(4, 0), do_bwd(2), ev_z(4, 1), do_bwd(3), ev_z(3, 2),
        do_bwd(4), ev_y(-3), ev_y(3), do_bwd(5), do_bwd(6), ev_z(4, 2), ev_y(-4), do_bwd(7),
    ]
    for step in plan:
        step()

    comm.phase = 1

    order = (4, -3, 3, -2, 2, -1, 1, 0)
    kinds = ((1, 0), (1, 1), (0, 0), (0, 1))
    core_got = {}
    for n, d in enumerate(order):
        slot = comm.slot()
        for m, (other, h) in enumerate(kinds):
            tile = ctile(other, d, h, 1 - core, -1)
            part[tile] = bwd_each[idx[5, tile]]
            comm.send(part.at[tile], from_core.at[4 * n + m], partner, slot=slot)
        four = from_core.at[pl.ds(4 * n, 4)]
        core_got[d] = (n, comm.copy(four, four, partner, slot).wait_recv)
    own_y, a_got, b_got = {}, {}, {}
    RPIECES = ((0, 0), (1, 0), (0, 1))

    def ring_send(p, d, sign, slot, got):
        other, h = RPIECES[p]
        got[p, slot] = comm.send(
            part.at[ctile(other, d, h)], ring.at[slot * 3 + p], za if sign > 0 else zb
        )

    def ev_merge(d):
        def run():
            n, wait = core_got[d]
            wait()
            for m, (other, h) in enumerate(kinds):
                tile = ctile(other, d, h)
                part[tile] = bwd_each[idx[5, tile]] + from_core[4 * n + m]
                if (other, h) == (1, 1):
                    own_y[d] = comm.send(part.at[tile], from_y.at[d % NZ], ypair)
                if d == 4 and h == 0:
                    ring_send(other, 4, 1, 3, a_got)
                if d == -3 and h == 0:
                    ring_send(other, -3, -1, 6, b_got)

        return run

    def ev_merge_y(d):
        def run():
            own_y[d]()
            tile = ctile(0, d, 1)
            part[tile] = part[tile] + from_y[d % NZ]
            if d == 4:
                ring_send(2, 4, 1, 3, a_got)
            if d == -3:
                ring_send(2, -3, -1, 6, b_got)

        return run

    def ev_a(p, left):
        def run():
            other, h = RPIECES[p]
            a_got[p, left]()
            tile = ctile(other, left, h)
            part[tile] = part[tile] + ring[left * 3 + p]
            if left:
                ring_send(p, left, 1, left - 1, a_got)

        return run

    def ev_b(p, left):
        def run():
            other, h = RPIECES[p]
            b_got[p, 4 + left]()
            tile = ctile(other, -left, h)
            part[tile] = part[tile] + ring[(4 + left) * 3 + p]
            if left:
                ring_send(p, -left, -1, 4 + left - 1, b_got)

        return run

    def ev_grad_y():
        own_y["end"] = comm.send(part.at[ctile(1, 0, 0)], from_y.at[NZ], ypair)

    def ev_grad(h):
        def run():
            total = part[ctile(0, 0, h)]
            if h == 0:
                own_y["end"]()
                total = total + from_y[NZ]
            cs = lax.rsqrt(cdeg[pl.ds(h, 1), :].astype(F32))
            out[2 + h] = (total * cs).T

        return run

    fa, fb = {}, {}

    def two(ref, tile):
        return ref.at[pl.ds(tile, 2)]

    def ev_f_start():
        for other in (1, 0):
            for d in (2, -1, 1, 0):
                for h in range(2):
                    tile = rtile(other, d, h)
                    fpart[tile] = fwd_each[idx[4, tile]]
                if d == 2:
                    fa[other] = comm.send(two(fpart, rtile(other, 2, 0)), two(xring, other * 2), xa, n=2)
                if d == -1:
                    fb[other] = comm.send(two(fpart, rtile(other, -1, 0)), two(xring, 4 + other * 2), xb, n=2)

    def ev_f_mid(other):
        def run():
            fa[other]()
            for h in range(2):
                tile = rtile(other, 1, h)
                fpart[tile] = fpart[tile] + xring[other * 2 + h]
            fa[other] = comm.send(two(fpart, rtile(other, 1, 0)), two(xring, 8 + other * 2), xa, n=2)

        return run

    def ev_f_last(other):
        def run():
            fb[other]()
            fa[other]()
            for h in range(2):
                tile = rtile(other, 0, h)
                fpart[tile] = fpart[tile] + (xring[4 + other * 2 + h] + xring[8 + other * 2 + h])
            if other:
                fa["y"] = comm.send(two(fpart, rtile(1, 0, 0)), two(from_yh, 0), ypeer, n=2)

        return run

    def ev_f_end():
        fa["y"]()
        for h in range(2):
            rs = lax.rsqrt(rdeg[pl.ds(h, 1), :].astype(F32))
            total = fpart[rtile(0, 0, h)] + from_yh[h]
            out[h] = (total.T * rs).T

    plan = [
        ev_core_end, ev_merge(4), ev_merge(-3), do_ssplit, ev_merge(3), ev_merge(-2), do_fwd(0),
        ev_merge(2), ev_merge(-1), ev_merge(1), ev_merge(0), do_fwd(1),
        ev_a(1, 3), ev_b(1, 2), ev_merge_y(4), do_fwd(2), ev_a(0, 3), ev_b(0, 2), ev_merge_y(-3), do_fwd(3),
        ev_merge_y(3), do_fwd(4), ev_a(2, 3), ev_merge_y(-2), do_fwd(5),
        ev_a(1, 2), ev_b(1, 1), ev_b(2, 2), do_fwd(6), ev_a(0, 2), ev_b(0, 1), ev_merge_y(2), ev_merge_y(-1), do_fwd(7),
        ev_f_start, ev_a(2, 2), ev_merge_y(1), ev_a(1, 1), ev_b(1, 0), ev_b(2, 1), ev_merge_y(0),
        ev_a(0, 1), ev_b(0, 0), ev_f_mid(1), ev_f_mid(0), ev_a(2, 1), ev_a(1, 0), ev_grad_y, ev_b(2, 0),
        ev_f_last(1), ev_a(0, 0), ev_f_last(0), ev_a(2, 0), ev_grad(1), ev_grad(0), ev_f_end,
    ]
    for step in plan:
        step()
    assert comm.tiles == [N_AG, N_RS] and comm.n == N_RECV, (comm.tiles, comm.n)
    for phase, n in ((0, N_AG), (1, N_RS)):
        comm.phase = phase
        comm.copy(fwd_each.at[pl.ds(0, n)], fwd_each.at[pl.ds(0, n)], partner, 0).wait_send()


def per_device(embed, cotangent, tile_values, tile_coords, tile_count, row_degree, col_degree):
    vmem = pl.BlockSpec(memory_space=pltpu.VMEM)
    anywhere = pl.BlockSpec(memory_space=pl.ANY)
    tile = lambda n, dtype=F32, a=T, b=T: pltpu.VMEM((n, a, b), dtype)
    ints = lambda n: pltpu.VMEM((n, T), jnp.int32)
    out = pl.pallas_call(
        kernel,
        out_shape=jax.ShapeDtypeStruct((4, T, T), F32),
        in_specs=[anywhere] * 7,
        out_specs=vmem,
        scratch_shapes=[
            pltpu.VMEM((2 * T, T), F32), pltpu.VMEM((2 * T, T), F32), ints(2), ints(2), ints(2),
            pltpu.SMEM((1, 1), jnp.int32), ints(8), pltpu.SMEM((8, T), jnp.int32),
            tile(64), tile(64, BF16, T, 2 * T), tile(SLOTS), tile(SLOTS, BF16, 2 * T, T),
            tile(SLOTS + 1), tile(SLOTS + 1), tile(64), tile(32), tile(21), tile(9),
            tile(16), tile(16, BF16, 2 * T, T), tile(16), tile(12), tile(2),
            pltpu.SemaphoreType.DMA((2,)),
            pltpu.SemaphoreType.DMA((N_RECV,)),
            pltpu.SemaphoreType.DMA((11,)),
        ],
        compiler_params=pltpu.CompilerParams(
            collective_id=0, has_side_effects=True, vmem_limit_bytes=VMEM_LIMIT
        ),
    )(
        embed, cotangent, row_degree.reshape(2, T), col_degree.reshape(2, T),
        tile_coords.reshape(2, T), tile_count, tile_values[0, 0],
    )
    return out[:2].reshape(2 * T, T), out[2:].reshape(2 * T, T)


def solution(mesh):
    return jax.shard_map(
        per_device,
        mesh=mesh,
        in_specs=(
            P(("row", "col"), None),
            P(("col", "row"), None),
            P("col", "row", None, None, None),
            P(None, "col", "row", None),
            P("col", "row"),
            P(("col", "row")),
            P(("row", "col")),
        ),
        out_specs=(P(("col", "row"), None), P(("row", "col"), None)),
        check_vma=False,
    )
```

```python
import jax
import jax.numpy as jnp
from jax import lax
from jax.experimental import pallas as pl
from jax.experimental.pallas import tpu as pltpu
from jax.sharding import PartitionSpec as P

MESH = pl.DeviceIdType.MESH
F32 = jnp.float32
BF16 = jnp.bfloat16
T = 128
SLOTS = 128
NX, NZ = 4, 8
UNROLL = 16
VMEM_LIMIT = 58 * 1024 * 1024
N_RECV = 97
N_AG = N_RS = 76


class Comm:
    def __init__(self, send_sem, recv_sems):
        self.send_sem, self.recv_sems, self.n, self.tiles = send_sem, recv_sems, 0, [0, 0]

    def slot(self):
        self.n += 1
        return self.n - 1

    def copy(self, src, dst, dev, slot, phase=0):
        return pltpu.make_async_remote_copy(
            src_ref=src,
            dst_ref=dst,
            send_sem=self.send_sem.at[phase],
            recv_sem=self.recv_sems.at[slot],
            device_id=dev,
            device_id_type=MESH,
        )

    def send(self, src, dst, dev, land=None, slot=None, phase=0):
        slot = self.slot() if slot is None else slot
        self.copy(src, dst, dev, slot, phase).start()
        self.tiles[phase] += 1
        return lambda: self.copy(src, dst if land is None else land, dev, slot).wait_recv()


def split(value):
    high = value.astype(BF16)
    return high, (value - high.astype(F32)).astype(BF16)


def kernel(
    embed_hbm, cot_hbm, rdeg_hbm, cdeg_hbm, coords_hbm, count_hbm, values,
    out,
    embed, cot, rdeg, cdeg, coords, count, table, idx,
    panel, pairs, vraw, vpair, fwd_each, bwd_each, part, from_core, ring, from_y,
    gpanel, gpair, fpart, xring, from_yh,
    send_sem, recv_sems, load_sems,
):
    row, col = lax.axis_index("row"), lax.axis_index("col")
    x, yh = lax.div(row, 2), lax.rem(row, 2)
    core, chip = lax.rem(col, 2), lax.div(col, 2)
    yl, z = lax.div(chip, NZ), lax.rem(chip, NZ)
    turn = 1 - 2 * core

    def zat(d):
        return lax.rem(z + turn * d + NZ, NZ)

    def xat(d):
        return lax.rem(x + turn * d + NX, NX)

    def colof(y, zz, c):
        return (y * NZ + zz) * 2 + c

    def ctile(other, d, h, c=None, sign=1):
        y = 1 - yl if other else yl
        return colof(y, zat(sign * d), core if c is None else c) * 2 + h

    def rtile(other, d, h):
        return (xat(d) * 2 + (1 - yh if other else yh)) * 2 + h

    partner = (row, col + turn)
    za = (row, colof(yl, zat(1), core))
    zb = (row, colof(yl, zat(-1), core))
    ypair = (row, colof(1 - yl, z, core))
    ypeer = (x * 2 + 1 - yh, col)
    xa = (xat(1) * 2 + yh, col)
    xb = (xat(-1) * 2 + yh, col)

    barrier = pltpu.get_barrier_semaphore()
    for dev in (za, zb, xa, xb, ypair, ypeer, partner):
        pl.semaphore_signal(barrier, inc=1, device_id=dev, device_id_type=MESH)

    inputs = []
    for n, (src, dst) in enumerate((
        (cot_hbm, cot), (rdeg_hbm, rdeg), (embed_hbm, embed), (cdeg_hbm, cdeg), (coords_hbm, coords), (count_hbm, count)
    )):
        load = pltpu.make_async_copy(src, dst, load_sems.at[n])
        load.start()
        inputs.append(load)
    loads = []
    group = SLOTS // 8
    for g in range(4):
        piece = pl.ds(g * 2 * group, 2 * group)
        load = pltpu.make_async_copy(values.at[piece], vraw.at[piece], load_sems.at[6 + g])
        load.start()
        loads.append(load)
    for load in inputs:
        load.wait()

    for h in range(2):
        half = pl.ds(h * T, T)
        rs = lax.rsqrt(rdeg[pl.ds(h, 1), :].astype(F32))
        cs = lax.rsqrt(cdeg[pl.ds(h, 1), :].astype(F32))
        gpanel[rtile(0, 0, h)] = cot[half, :].T * rs
        panel[ctile(0, 0, h)] = (embed[half, :].T * cs).T
    pl.semaphore_wait(barrier, 7)

    comm = Comm(send_sem, recv_sems)

    def share(ref, tile, dev, land):
        return comm.send(ref.at[tile], ref.at[tile], dev, ref.at[land])

    def push(src, dst, dev, slot=None):
        return comm.send(src, dst, dev, slot=slot, phase=1)

    core_slot = comm.slot()

    def col_core(tile):
        comm.send(panel.at[tile], panel.at[tile], partner, slot=core_slot)

    got_yh, xa1, xb1, xa2 = {}, {}, {}, {}

    def x_send(other, h):
        xa1[other, h] = share(gpanel, rtile(other, 0, h), xa, rtile(other, -1, h))
        xb1[other, h] = share(gpanel, rtile(other, 0, h), xb, rtile(other, 1, h))

    x_send(0, 0)
    x_send(0, 1)
    got_yh[0] = share(gpanel, rtile(0, 0, 0), ypeer, rtile(1, 0, 0))
    za_got, zb_got, y_got = {}, {}, {}
    PIECES = ((0, 0), (0, 1), (1, 0))

    def z_send(p, k):
        other, h = PIECES[p]
        if k < 4:
            za_got[k + 1, p] = share(panel, ctile(other, -k, h), za, ctile(other, -k - 1, h))
        if k < 3:
            zb_got[k + 1, p] = share(panel, ctile(other, k, h), zb, ctile(other, k + 1, h))

    z_send(0, 0)
    y_first = share(panel, ctile(0, 0, 0), ypair, ctile(1, 0, 0))
    got_yh[1] = share(gpanel, rtile(0, 0, 1), ypeer, rtile(1, 0, 1))
    z_send(1, 0)
    y_got[0] = share(panel, ctile(0, 0, 1), ypair, ctile(1, 0, 1))
    for h in range(2):
        col_core(ctile(0, 0, h))

    sub = lax.broadcasted_iota(jnp.int32, (T, T), 0)
    lane = lax.broadcasted_iota(jnp.int32, (T, T), 1)
    live = sub < count[0, 0]

    def latest(hit):
        best = jnp.max(jnp.where(hit & live, sub, -1), axis=0, keepdims=True)
        return jnp.where(best < 0, SLOTS, best)

    for n in range(2):
        key = jnp.broadcast_to(coords[pl.ds(n, 1), :], (T, T))
        down = key.T
        table[pl.ds(n, 1), :] = coords[pl.ds(n, 1), :]
        table[pl.ds(2 + n, 1), :] = latest((down == key) & (sub < lane))
        table[pl.ds(4 + n, 1), :] = latest(down == lane)
    to_smem = pltpu.make_async_copy(table, idx, load_sems.at[10])
    to_smem.start()
    fwd_each[SLOTS] = jnp.zeros((T, T), F32)
    bwd_each[SLOTS] = jnp.zeros((T, T), F32)

    def ev_row_y(h):
        def run():
            got_yh[h]()
            x_send(1, h)

        return run

    def ev_x(other, h):
        def run():
            xa1[other, h]()
            xa2[other, h] = share(gpanel, rtile(other, -1, h), xa, rtile(other, -2, h))
            xb1[other, h]()

        return run

    def ev_x_end():
        for key in ((0, 0), (0, 1), (1, 0), (1, 1)):
            xa2[key]()

    def ev_y_first():
        y_first()
        z_send(2, 0)
        col_core(ctile(1, 0, 0))

    def ev_z(k, p):
        def run():
            other, h = PIECES[p]
            za_got[k, p]()
            if k < 4:
                zb_got[k, p]()
                z_send(p, k)
            for s in (-1, 1) if k < 4 else (-1,):
                tile = ctile(other, s * k, h)
                if p == 1:
                    y_got[s * k] = share(panel, tile, ypair, ctile(1, s * k, 1))
                col_core(tile)

        return run

    def ev_y(d):
        def run():
            y_got[d]()
            col_core(ctile(1, d, 1))

        return run

    def ev_core_end():
        comm.copy(panel.at[pl.ds(0, 32)], panel.at[pl.ds(0, 32)], partner, core_slot).wait_recv()

    def do_split(g):
        def run():
            if g % 2 == 0:
                loads[g // 2].wait()

            def body(i, carry):
                for u in range(2):
                    t = g * group + i * 2 + u
                    high, low = split(vraw[t])
                    vpair[t, pl.ds(0, T), :] = high
                    vpair[t, pl.ds(T, T), :] = low
                return carry

            lax.fori_loop(0, group // 2, body, 0)

        return run

    def do_gsplit():
        to_smem.wait()

        def body(r, carry):
            high, low = split(gpanel[r])
            gpair[r, pl.ds(0, T), :] = high
            gpair[r, pl.ds(T, T), :] = low
            return carry

        lax.fori_loop(0, 4 * NX, body, 0)

    def do_bwd(g):
        def run():
            def body(i, carry):
                for u in range(UNROLL):
                    t = g * group + i * UNROLL + u
                    g2 = gpair[idx[0, t]]
                    res = jnp.dot(
                        jnp.concatenate([g2, g2], axis=1), vpair[t], preferred_element_type=F32
                    )
                    bwd_each[t] = res[:T] + res[T:] + bwd_each[idx[3, t]]
                return carry

            lax.fori_loop(0, group // UNROLL, body, 0)

        return run

    def do_ssplit():
        def body(c, carry):
            for u in range(2):
                high, low = split(panel[c * 2 + u])
                pairs[c * 2 + u, :, pl.ds(0, T)] = high
                pairs[c * 2 + u, :, pl.ds(T, T)] = low
            return carry

        lax.fori_loop(0, 4 * NZ, body, 0)

    def do_fwd(g):
        def run():
            def body(i, carry):
                for u in range(UNROLL):
                    t = g * group + i * UNROLL + u
                    s2 = pairs[idx[1, t]]
                    v2 = jnp.concatenate([vpair[t, pl.ds(0, T), :], vpair[t, pl.ds(T, T), :]], axis=1)
                    res = jnp.dot(
                        v2, jnp.concatenate([s2, s2], axis=0), preferred_element_type=F32
                    )
                    fwd_each[t] = res[:, :T] + res[:, T:] + fwd_each[idx[2, t]]
                return carry

            lax.fori_loop(0, group // UNROLL, body, 0)

        return run

    order = (4, -3, 3, -2, 2, -1, 1, 0)
    kinds = ((1, 0), (1, 1), (0, 0), (0, 1))
    core_got = {}

    def ev_pick(d):
        def run():
            n, slot = order.index(d), comm.slot()
            for m, (other, h) in enumerate(kinds):
                tile = ctile(other, d, h, 1 - core, -1)
                part[tile] = bwd_each[idx[5, tile]]
                push(part.at[tile], from_core.at[4 * n + m], partner, slot)
            four = from_core.at[pl.ds(4 * n, 4)]
            core_got[d] = (n, lambda: comm.copy(four, four, partner, slot).wait_recv())

        return run

    own_y, a_got, b_got = {}, {}, {}
    RPIECES = ((0, 0), (1, 0), (0, 1))

    def ring_send(p, d, sign, slot, got):
        other, h = RPIECES[p]
        got[p, slot] = push(
            part.at[ctile(other, d, h)], ring.at[slot * 3 + p], za if sign > 0 else zb
        )

    def ev_merge(d):
        def run():
            n, wait = core_got[d]
            wait()
            for m, (other, h) in enumerate(kinds):
                tile = ctile(other, d, h)
                part[tile] = bwd_each[idx[5, tile]] + from_core[4 * n + m]
                if (other, h) == (1, 1):
                    own_y[d] = push(part.at[tile], from_y.at[d % NZ], ypair)
                if d == 4 and h == 0:
                    ring_send(other, 4, 1, 3, a_got)
                if d == -3 and h == 0:
                    ring_send(other, -3, -1, 6, b_got)

        return run

    def ev_merge_y(d):
        def run():
            own_y[d]()
            tile = ctile(0, d, 1)
            part[tile] = part[tile] + from_y[d % NZ]
            if d == 4:
                ring_send(2, 4, 1, 3, a_got)
            if d == -3:
                ring_send(2, -3, -1, 6, b_got)

        return run

    def ev_a(p, left):
        def run():
            other, h = RPIECES[p]
            a_got[p, left]()
            tile = ctile(other, left, h)
            part[tile] = part[tile] + ring[left * 3 + p]
            if left:
                ring_send(p, left, 1, left - 1, a_got)

        return run

    def ev_b(p, left):
        def run():
            other, h = RPIECES[p]
            b_got[p, 4 + left]()
            tile = ctile(other, -left, h)
            part[tile] = part[tile] + ring[(4 + left) * 3 + p]
            if left:
                ring_send(p, -left, -1, 4 + left - 1, b_got)

        return run

    def ev_grad_y():
        own_y["end"] = push(part.at[ctile(1, 0, 0)], from_y.at[NZ], ypair)

    def ev_grad(h):
        def run():
            total = part[ctile(0, 0, h)]
            if h == 0:
                own_y["end"]()
                total = total + from_y[NZ]
            cs = lax.rsqrt(cdeg[pl.ds(h, 1), :].astype(F32))
            out[2 + h] = (total * cs).T

        return run

    fa, fb, fy = {}, {}, {}

    def f_a2(other, h):
        fa[other, h] = push(fpart.at[rtile(other, 2, h)], xring.at[other * 2 + h], xa)

    def f_b1(other, h):
        fb[other, h] = push(fpart.at[rtile(other, -1, h)], xring.at[4 + other * 2 + h], xb)

    def ev_f_start():
        for other, d in ((1, 2), (1, -1), (0, 2), (0, -1), (1, 1), (0, 1), (1, 0), (0, 0)):
            for h in range(2):
                tile = rtile(other, d, h)
                fpart[tile] = fwd_each[idx[4, tile]]
            for h in range(2):
                if d == 2:
                    f_a2(other, h)
                if (other, d) == (1, -1):
                    f_b1(other, h)

    def ev_f_mid(other, h):
        def run():
            fa[other, h]()
            tile = rtile(other, 1, h)
            fpart[tile] = fpart[tile] + xring[other * 2 + h]
            fa[other, h] = push(fpart.at[tile], xring.at[8 + other * 2 + h], xa)
            if (other, h) == (1, 1):
                f_b1(0, 0)
                f_b1(0, 1)

        return run

    def ev_f_last(other, h):
        def run():
            fb[other, h]()
            fa[other, h]()
            tile = rtile(other, 0, h)
            fpart[tile] = fpart[tile] + (xring[4 + other * 2 + h] + xring[8 + other * 2 + h])
            if other:
                fy[h] = push(fpart.at[tile], from_yh.at[h], ypeer)

        return run

    def ev_f_end(h):
        def run():
            fy[h]()
            rs = lax.rsqrt(rdeg[pl.ds(h, 1), :].astype(F32))
            total = fpart[rtile(0, 0, h)] + from_yh[h]
            out[h] = (total.T * rs).T

        return run

    plan = [
        do_split(0), do_split(1), do_split(2), do_split(3), do_split(4), do_split(5), ev_x(0, 0), ev_z(1, 0),
        do_split(6), do_split(7), ev_row_y(0), ev_y_first, ev_x(0, 1), ev_z(1, 1), ev_row_y(1), ev_y(0),
        ev_z(2, 0), ev_x(1, 0), ev_y(-1), ev_z(1, 2), ev_y(1), ev_z(2, 1), ev_x(1, 1), ev_z(3, 0), ev_z(2, 2),
        ev_x_end, do_gsplit, ev_y(-2), do_bwd(0), do_bwd(1), ev_z(3, 1), do_bwd(2), ev_z(4, 0), ev_y(2),
        do_bwd(3), do_bwd(4), do_bwd(5), do_bwd(6), ev_z(3, 2), do_bwd(7), ev_pick(4), ev_pick(-3), ev_pick(3),
        ev_pick(-2), ev_pick(2), ev_z(4, 1), ev_pick(-1), ev_pick(1), ev_pick(0), ev_y(-3), ev_merge(4),
        ev_merge(-3), ev_y(3), ev_merge(3), ev_merge(-2), ev_z(4, 2), ev_merge(2), ev_merge(-1), ev_y(-4),
        ev_merge(1), ev_merge(0), ev_a(1, 3), ev_core_end, do_ssplit, do_fwd(0), ev_merge_y(4), ev_a(0, 3),
        do_fwd(1), do_fwd(2), do_fwd(3), do_fwd(4), do_fwd(5), do_fwd(6), do_fwd(7), ev_f_start, ev_a(1, 2),
        ev_merge_y(3), ev_merge_y(-2), ev_a(2, 3), ev_merge_y(-3), ev_b(1, 2), ev_b(0, 2), ev_a(0, 2),
        ev_merge_y(2), ev_merge_y(-1), ev_f_mid(1, 0), ev_a(1, 1), ev_merge_y(1), ev_f_mid(1, 1), ev_a(2, 2),
        ev_b(2, 2), ev_merge_y(0), ev_b(1, 1), ev_f_mid(0, 0), ev_b(0, 1), ev_f_mid(0, 1), ev_a(0, 1),
        ev_f_last(1, 0), ev_a(1, 0), ev_f_last(1, 1), ev_a(2, 1), ev_b(2, 1), ev_b(1, 0), ev_grad_y,
        ev_f_last(0, 0), ev_b(0, 0), ev_f_last(0, 1), ev_a(0, 0), ev_a(2, 0), ev_f_end(0), ev_b(2, 0),
        ev_grad(1), ev_f_end(1), ev_grad(0),
    ]
    for step in plan:
        step()
    assert comm.tiles == [N_AG, N_RS] and comm.n == N_RECV, (comm.tiles, comm.n)
    for phase, n in ((0, N_AG), (1, N_RS)):
        comm.copy(fwd_each.at[pl.ds(0, n)], fwd_each.at[pl.ds(0, n)], partner, 0, phase).wait_send()


def per_device(embed, cotangent, tile_values, tile_coords, tile_count, row_degree, col_degree):
    vmem = pl.BlockSpec(memory_space=pltpu.VMEM)
    anywhere = pl.BlockSpec(memory_space=pl.ANY)
    tile = lambda n, dtype=F32, a=T, b=T: pltpu.VMEM((n, a, b), dtype)
    ints = lambda n: pltpu.VMEM((n, T), jnp.int32)
    out = pl.pallas_call(
        kernel,
        out_shape=jax.ShapeDtypeStruct((4, T, T), F32),
        in_specs=[anywhere] * 7,
        out_specs=vmem,
        scratch_shapes=[
            pltpu.VMEM((2 * T, T), F32), pltpu.VMEM((2 * T, T), F32), ints(2), ints(2), ints(2),
            pltpu.SMEM((1, 1), jnp.int32), ints(8), pltpu.SMEM((8, T), jnp.int32),
            tile(64), tile(64, BF16, T, 2 * T), tile(SLOTS), tile(SLOTS, BF16, 2 * T, T),
            tile(SLOTS + 1), tile(SLOTS + 1), tile(64), tile(32), tile(21), tile(9),
            tile(16), tile(16, BF16, 2 * T, T), tile(16), tile(12), tile(2),
            pltpu.SemaphoreType.DMA((2,)),
            pltpu.SemaphoreType.DMA((N_RECV,)),
            pltpu.SemaphoreType.DMA((11,)),
        ],
        compiler_params=pltpu.CompilerParams(
            collective_id=0, has_side_effects=True, vmem_limit_bytes=VMEM_LIMIT
        ),
    )(
        embed, cotangent, row_degree.reshape(2, T), col_degree.reshape(2, T),
        tile_coords.reshape(2, T), tile_count, tile_values[0, 0],
    )
    return out[:2].reshape(2 * T, T), out[2:].reshape(2 * T, T)


def solution(mesh):
    return jax.shard_map(
        per_device,
        mesh=mesh,
        in_specs=(
            P(("row", "col"), None),
            P(("col", "row"), None),
            P("col", "row", None, None, None),
            P(None, "col", "row", None),
            P("col", "row"),
            P(("col", "row")),
            P(("row", "col")),
        ),
        out_specs=(P(("col", "row"), None), P(("row", "col"), None)),
        check_vma=False,
    )
```

```python
import jax
import jax.numpy as jnp
from jax import lax
from jax.experimental import pallas as pl
from jax.experimental.pallas import tpu as pltpu
from jax.sharding import PartitionSpec as P

MESH = pl.DeviceIdType.MESH
F32 = jnp.float32
BF16 = jnp.bfloat16
T = 128
SLOTS = 128
NX, NZ = 4, 8
UNROLL = 16
VMEM_LIMIT = 53 * 1024 * 1024
N_RECV = 97
N_AG = N_RS = 76


class Comm:
    def __init__(self, send_sem, recv_sems):
        self.send_sem, self.recv_sems, self.n, self.tiles = send_sem, recv_sems, 0, [0, 0]

    def slot(self):
        self.n += 1
        return self.n - 1

    def copy(self, src, dst, dev, slot, phase=0):
        return pltpu.make_async_remote_copy(
            src_ref=src,
            dst_ref=dst,
            send_sem=self.send_sem.at[phase],
            recv_sem=self.recv_sems.at[slot],
            device_id=dev,
            device_id_type=MESH,
        )

    def send(self, src, dst, dev, land=None, slot=None, phase=0):
        slot = self.slot() if slot is None else slot
        self.copy(src, dst, dev, slot, phase).start()
        self.tiles[phase] += 1
        return lambda: self.copy(src, dst if land is None else land, dev, slot).wait_recv()


def split(value):
    high = value.astype(BF16)
    return high, (value - high.astype(F32)).astype(BF16)


def kernel(
    embed_hbm, cot_hbm, rdeg_hbm, cdeg_hbm, coords_hbm, count_hbm, values,
    out_hbm,
    embed, cot, rdeg, cdeg, coords, count, table, idx,
    panel, pairs, vraw, vpair, fwd_each, bwd_each, part, from_core, ring, from_y,
    gpanel, gpair, fpart, xring, from_yh,
    out, send_sem, recv_sems, load_sems,
):
    row, col = lax.axis_index("row"), lax.axis_index("col")
    x, yh = lax.div(row, 2), lax.rem(row, 2)
    core, chip = lax.rem(col, 2), lax.div(col, 2)
    yl, z = lax.div(chip, NZ), lax.rem(chip, NZ)
    turn = 1 - 2 * core

    def zat(d):
        return lax.rem(z + turn * d + NZ, NZ)

    def xat(d):
        return lax.rem(x + turn * d + NX, NX)

    def colof(y, zz, c):
        return (y * NZ + zz) * 2 + c

    def ctile(other, d, h, c=None, sign=1):
        y = 1 - yl if other else yl
        return colof(y, zat(sign * d), core if c is None else c) * 2 + h

    def rtile(other, d, h):
        return (xat(d) * 2 + (1 - yh if other else yh)) * 2 + h

    partner = (row, col + turn)
    za = (row, colof(yl, zat(1), core))
    zb = (row, colof(yl, zat(-1), core))
    ypair = (row, colof(1 - yl, z, core))
    ypeer = (x * 2 + 1 - yh, col)
    xa = (xat(1) * 2 + yh, col)
    xb = (xat(-1) * 2 + yh, col)

    barrier = pltpu.get_barrier_semaphore()
    for dev in (za, zb, xa, xb, ypair, ypeer, partner):
        pl.semaphore_signal(barrier, inc=1, device_id=dev, device_id_type=MESH)

    inputs = []
    for n, (src, dst) in enumerate((
        (cot_hbm, cot), (rdeg_hbm, rdeg), (embed_hbm, embed), (cdeg_hbm, cdeg), (coords_hbm, coords), (count_hbm, count)
    )):
        load = pltpu.make_async_copy(src, dst, load_sems.at[n])
        load.start()
        inputs.append(load)
    loads = []
    group = SLOTS // 8
    for g in range(4):
        piece = pl.ds(g * 2 * group, 2 * group)
        load = pltpu.make_async_copy(values.at[piece], vraw.at[piece], load_sems.at[6 + g])
        load.start()
        loads.append(load)
    for load in inputs:
        load.wait()

    for h in range(2):
        half = pl.ds(h * T, T)
        rs = lax.rsqrt(rdeg[pl.ds(h, 1), :].astype(F32))
        cs = lax.rsqrt(cdeg[pl.ds(h, 1), :].astype(F32))
        gpanel[rtile(0, 0, h)] = cot[half, :].T * rs
        panel[ctile(0, 0, h)] = (embed[half, :].T * cs).T
    pl.semaphore_wait(barrier, 7)

    comm = Comm(send_sem, recv_sems)

    def share(ref, tile, dev, land):
        return comm.send(ref.at[tile], ref.at[tile], dev, ref.at[land])

    def push(src, dst, dev, slot=None):
        return comm.send(src, dst, dev, slot=slot, phase=1)

    core_slot = comm.slot()

    def col_core(tile):
        comm.send(panel.at[tile], panel.at[tile], partner, slot=core_slot)

    got_yh, xa1, xb1, xa2 = {}, {}, {}, {}

    def x_send(other, h):
        xa1[other, h] = share(gpanel, rtile(other, 0, h), xa, rtile(other, -1, h))
        xb1[other, h] = share(gpanel, rtile(other, 0, h), xb, rtile(other, 1, h))

    x_send(0, 0)
    x_send(0, 1)
    y_first = share(panel, ctile(0, 0, 0), ypair, ctile(1, 0, 0))
    got_yh[0] = share(gpanel, rtile(0, 0, 0), ypeer, rtile(1, 0, 0))
    za_got, zb_got, y_got = {}, {}, {}
    PIECES = ((0, 0), (0, 1), (1, 0))

    def z_send(p, k):
        other, h = PIECES[p]
        if k < 4:
            za_got[k + 1, p] = share(panel, ctile(other, -k, h), za, ctile(other, -k - 1, h))
        if k < 3:
            zb_got[k + 1, p] = share(panel, ctile(other, k, h), zb, ctile(other, k + 1, h))

    got_yh[1] = share(gpanel, rtile(0, 0, 1), ypeer, rtile(1, 0, 1))
    z_send(1, 0)
    z_send(0, 0)
    y_got[0] = share(panel, ctile(0, 0, 1), ypair, ctile(1, 0, 1))
    for h in range(2):
        col_core(ctile(0, 0, h))

    sub = lax.broadcasted_iota(jnp.int32, (T, T), 0)
    lane = lax.broadcasted_iota(jnp.int32, (T, T), 1)
    live = sub < count[0, 0]

    def latest(hit):
        best = jnp.max(jnp.where(hit & live, sub, -1), axis=0, keepdims=True)
        return jnp.where(best < 0, SLOTS, best)

    for n in range(2):
        key = jnp.broadcast_to(coords[pl.ds(n, 1), :], (T, T))
        down = key.T
        table[pl.ds(n, 1), :] = coords[pl.ds(n, 1), :]
        table[pl.ds(2 + n, 1), :] = latest((down == key) & (sub < lane))
        table[pl.ds(4 + n, 1), :] = latest(down == lane)
    to_smem = pltpu.make_async_copy(table, idx, load_sems.at[10])
    to_smem.start()
    fwd_each[SLOTS] = jnp.zeros((T, T), F32)
    bwd_each[SLOTS] = jnp.zeros((T, T), F32)

    def ev_row_y(h):
        def run():
            got_yh[h]()
            x_send(1, h)

        return run

    def ev_x(other, h):
        def run():
            xa1[other, h]()
            xa2[other, h] = share(gpanel, rtile(other, -1, h), xa, rtile(other, -2, h))
            xb1[other, h]()

        return run

    def ev_x_end():
        for key in ((0, 0), (0, 1), (1, 0), (1, 1)):
            xa2[key]()

    def ev_y_first():
        y_first()
        z_send(2, 0)
        col_core(ctile(1, 0, 0))

    def ev_z(k, p):
        def run():
            other, h = PIECES[p]
            za_got[k, p]()
            if k < 4:
                zb_got[k, p]()
                z_send(p, k)
            for s in (-1, 1) if k < 4 else (-1,):
                tile = ctile(other, s * k, h)
                if p == 1:
                    y_got[s * k] = share(panel, tile, ypair, ctile(1, s * k, 1))
                col_core(tile)

        return run

    def ev_y(d):
        def run():
            y_got[d]()
            col_core(ctile(1, d, 1))

        return run

    def ev_core_end():
        comm.copy(panel.at[pl.ds(0, 32)], panel.at[pl.ds(0, 32)], partner, core_slot).wait_recv()

    def do_split(g):
        def run():
            if g % 2 == 0:
                loads[g // 2].wait()

            def body(i, carry):
                for u in range(2):
                    t = g * group + i * 2 + u
                    high, low = split(vraw[t])
                    vpair[t, pl.ds(0, T), :] = high
                    vpair[t, pl.ds(T, T), :] = low
                return carry

            lax.fori_loop(0, group // 2, body, 0)

        return run

    def do_gsplit():
        to_smem.wait()

        def body(r, carry):
            high, low = split(gpanel[r])
            gpair[r, pl.ds(0, T), :] = high
            gpair[r, pl.ds(T, T), :] = low
            return carry

        lax.fori_loop(0, 4 * NX, body, 0)

    def do_bwd(g):
        def run():
            def body(i, carry):
                for u in range(UNROLL):
                    t = g * group + i * UNROLL + u
                    g2 = gpair[idx[0, t]]
                    res = jnp.dot(
                        jnp.concatenate([g2, g2], axis=1), vpair[t], preferred_element_type=F32
                    )
                    bwd_each[t] = res[:T] + res[T:] + bwd_each[idx[3, t]]
                return carry

            lax.fori_loop(0, group // UNROLL, body, 0)

        return run

    def do_ssplit():
        def body(c, carry):
            for u in range(2):
                high, low = split(panel[c * 2 + u])
                pairs[c * 2 + u, :, pl.ds(0, T)] = high
                pairs[c * 2 + u, :, pl.ds(T, T)] = low
            return carry

        lax.fori_loop(0, 4 * NZ, body, 0)

    def do_fwd(g):
        def run():
            def body(i, carry):
                for u in range(UNROLL):
                    t = g * group + i * UNROLL + u
                    s2 = pairs[idx[1, t]]
                    v2 = jnp.concatenate([vpair[t, pl.ds(0, T), :], vpair[t, pl.ds(T, T), :]], axis=1)
                    res = jnp.dot(
                        v2, jnp.concatenate([s2, s2], axis=0), preferred_element_type=F32
                    )
                    fwd_each[t] = res[:, :T] + res[:, T:] + fwd_each[idx[2, t]]
                return carry

            lax.fori_loop(0, group // UNROLL, body, 0)

        return run

    order = (4, -3, 3, -2, 2, -1, 1, 0)
    kinds = ((1, 0), (1, 1), (0, 0), (0, 1))
    core_got = {}

    def ev_pick(d):
        def run():
            n, slot = order.index(d), comm.slot()
            for m, (other, h) in enumerate(kinds):
                tile = ctile(other, d, h, 1 - core, -1)
                part[tile] = bwd_each[idx[5, tile]]
                push(part.at[tile], from_core.at[4 * n + m], partner, slot)
            four = from_core.at[pl.ds(4 * n, 4)]
            core_got[d] = (n, lambda: comm.copy(four, four, partner, slot).wait_recv())

        return run

    own_y, a_got, b_got = {}, {}, {}
    RPIECES = ((0, 0), (1, 0), (0, 1))

    def ring_send(p, d, sign, slot, got):
        other, h = RPIECES[p]
        got[p, slot] = push(
            part.at[ctile(other, d, h)], ring.at[slot * 3 + p], za if sign > 0 else zb
        )

    def ev_merge(d):
        def run():
            n, wait = core_got[d]
            wait()
            for m, (other, h) in enumerate(kinds):
                tile = ctile(other, d, h)
                part[tile] = bwd_each[idx[5, tile]] + from_core[4 * n + m]
                if (other, h) == (1, 1):
                    own_y[d] = push(part.at[tile], from_y.at[d % NZ], ypair)
                if d == 4 and h == 0:
                    ring_send(other, 4, 1, 3, a_got)
                if d == -3 and h == 0:
                    ring_send(other, -3, -1, 6, b_got)

        return run

    def ev_merge_y(d):
        def run():
            own_y[d]()
            tile = ctile(0, d, 1)
            part[tile] = part[tile] + from_y[d % NZ]
            if d == 4:
                ring_send(2, 4, 1, 3, a_got)
            if d == -3:
                ring_send(2, -3, -1, 6, b_got)

        return run

    def ev_a(p, left):
        def run():
            other, h = RPIECES[p]
            a_got[p, left]()
            tile = ctile(other, left, h)
            part[tile] = part[tile] + ring[left * 3 + p]
            if left:
                ring_send(p, left, 1, left - 1, a_got)

        return run

    def ev_b(p, left):
        def run():
            other, h = RPIECES[p]
            b_got[p, 4 + left]()
            tile = ctile(other, -left, h)
            part[tile] = part[tile] + ring[(4 + left) * 3 + p]
            if left:
                ring_send(p, -left, -1, 4 + left - 1, b_got)

        return run

    def finish(n):
        copy = pltpu.make_async_copy(out.at[n], out_hbm.at[n], load_sems.at[n])
        copy.start()
        finished.append(copy)

    def ev_grad_y():
        own_y["end"] = push(part.at[ctile(1, 0, 0)], from_y.at[NZ], ypair)

    def ev_grad(h):
        def run():
            total = part[ctile(0, 0, h)]
            if h == 0:
                own_y["end"]()
                total = total + from_y[NZ]
            cs = lax.rsqrt(cdeg[pl.ds(h, 1), :].astype(F32))
            out[2 + h] = (total * cs).T
            finish(2 + h)

        return run

    fa, fb, fy = {}, {}, {}

    def f_a2(other, h):
        fa[other, h] = push(fpart.at[rtile(other, 2, h)], xring.at[other * 2 + h], xa)

    def f_b1(other, h):
        fb[other, h] = push(fpart.at[rtile(other, -1, h)], xring.at[4 + other * 2 + h], xb)

    def ev_f_start():
        for other, d in ((1, 2), (1, -1), (0, 2), (0, -1), (1, 1), (0, 1), (1, 0), (0, 0)):
            for h in range(2):
                tile = rtile(other, d, h)
                fpart[tile] = fwd_each[idx[4, tile]]
            for h in range(2):
                if d == 2:
                    f_a2(other, h)
                if (other, d) == (1, -1):
                    f_b1(other, h)

    def ev_f_mid(other, h):
        def run():
            fa[other, h]()
            tile = rtile(other, 1, h)
            fpart[tile] = fpart[tile] + xring[other * 2 + h]
            fa[other, h] = push(fpart.at[tile], xring.at[8 + other * 2 + h], xa)
            if (other, h) == (1, 1):
                f_b1(0, 0)
                f_b1(0, 1)

        return run

    def ev_f_last(other, h):
        def run():
            fb[other, h]()
            fa[other, h]()
            tile = rtile(other, 0, h)
            fpart[tile] = fpart[tile] + (xring[4 + other * 2 + h] + xring[8 + other * 2 + h])
            if other:
                fy[h] = push(fpart.at[tile], from_yh.at[h], ypeer)

        return run

    def ev_f_end(h):
        def run():
            fy[h]()
            rs = lax.rsqrt(rdeg[pl.ds(h, 1), :].astype(F32))
            total = fpart[rtile(0, 0, h)] + from_yh[h]
            out[h] = (total.T * rs).T
            finish(h)

        return run

    finished = []

    plan = [
        ev_y_first, ev_z(1, 1), ev_x(0, 0), ev_z(1, 0), do_split(0), ev_row_y(0), do_split(1), ev_z(1, 2),
        ev_row_y(1), ev_z(2, 1), do_split(2), do_split(3), ev_x(0, 1), do_split(4), ev_x(1, 0), ev_z(2, 0),
        do_split(5), do_split(6), ev_y(0), do_split(7), ev_x(1, 1), ev_z(2, 2), ev_z(3, 1), ev_y(-1), ev_y(2),
        ev_y(1), ev_y(-2), ev_x_end, do_gsplit, do_bwd(0), do_bwd(1), ev_z(3, 0), do_bwd(2), ev_z(3, 2),
        do_bwd(3), ev_z(4, 1), do_bwd(4), ev_y(-3), do_bwd(5), do_bwd(6), do_bwd(7), ev_pick(4), ev_pick(-3),
        ev_y(3), ev_pick(3), ev_z(4, 0), ev_merge(4), ev_z(4, 2), ev_y(-4), ev_pick(-2), ev_merge(-3),
        ev_pick(2), ev_merge(3), ev_core_end, do_ssplit, do_fwd(0), do_fwd(1), do_fwd(2), do_fwd(3), ev_a(1, 3),
        do_fwd(4), ev_merge_y(4), do_fwd(5), ev_a(0, 3), do_fwd(6), do_fwd(7), ev_f_start, ev_merge(-2),
        ev_merge_y(-3), ev_pick(-1), ev_merge_y(3), ev_b(0, 2), ev_merge(2), ev_b(1, 2), ev_merge(-1),
        ev_pick(1), ev_a(2, 3), ev_a(1, 2), ev_pick(0), ev_merge(1), ev_a(0, 2), ev_merge_y(-2), ev_f_mid(1, 0),
        ev_f_mid(1, 1), ev_b(2, 2), ev_merge_y(2), ev_b(1, 1), ev_merge(0), ev_a(2, 2), ev_a(1, 1),
        ev_f_last(1, 0), ev_merge_y(-1), ev_b(0, 1), ev_b(2, 1), ev_merge_y(1), ev_f_last(1, 1), ev_f_mid(0, 0),
        ev_a(0, 1), ev_f_mid(0, 1), ev_b(1, 0), ev_a(2, 1), ev_merge_y(0), ev_a(1, 0), ev_grad_y, ev_a(0, 0),
        ev_b(2, 0), ev_f_last(0, 1), ev_b(0, 0), ev_f_last(0, 0), ev_f_end(0), ev_a(2, 0), ev_grad(1),
        ev_f_end(1), ev_grad(0),
    ]
    for step in plan:
        step()
    for copy in finished:
        copy.wait()
    assert comm.tiles == [N_AG, N_RS] and comm.n == N_RECV, (comm.tiles, comm.n)
    for phase, n in ((0, N_AG), (1, N_RS)):
        comm.copy(fwd_each.at[pl.ds(0, n)], fwd_each.at[pl.ds(0, n)], partner, 0, phase).wait_send()


def per_device(embed, cotangent, tile_values, tile_coords, tile_count, row_degree, col_degree):
    anywhere = pl.BlockSpec(memory_space=pl.ANY)
    hbm = lambda a: pltpu.with_memory_space_constraint(a, pltpu.HBM)
    tile = lambda n, dtype=F32, a=T, b=T: pltpu.VMEM((n, a, b), dtype)
    ints = lambda n: pltpu.VMEM((n, T), jnp.int32)
    out = pl.pallas_call(
        kernel,
        out_shape=jax.ShapeDtypeStruct((4, T, T), F32),
        in_specs=[anywhere] * 7,
        out_specs=anywhere,
        scratch_shapes=[
            pltpu.VMEM((2 * T, T), F32), pltpu.VMEM((2 * T, T), F32), ints(2), ints(2), ints(2),
            pltpu.SMEM((1, 1), jnp.int32), ints(8), pltpu.SMEM((8, T), jnp.int32),
            tile(64), tile(64, BF16, T, 2 * T), tile(SLOTS), tile(SLOTS, BF16, 2 * T, T),
            tile(SLOTS + 1), tile(SLOTS + 1), tile(64), tile(32), tile(21), tile(9),
            tile(16), tile(16, BF16, 2 * T, T), tile(16), tile(12), tile(2),
            tile(4),
            pltpu.SemaphoreType.DMA((2,)),
            pltpu.SemaphoreType.DMA((N_RECV,)),
            pltpu.SemaphoreType.DMA((11,)),
        ],
        compiler_params=pltpu.CompilerParams(
            collective_id=0, has_side_effects=True, vmem_limit_bytes=VMEM_LIMIT
        ),
    )(
        hbm(embed), hbm(cotangent), hbm(row_degree.reshape(2, T)), hbm(col_degree.reshape(2, T)),
        hbm(tile_coords.reshape(2, T)), tile_count, hbm(tile_values[0, 0]),
    )
    return out[:2].reshape(2 * T, T), out[2:].reshape(2 * T, T)


def solution(mesh):
    return jax.shard_map(
        per_device,
        mesh=mesh,
        in_specs=(
            P(("row", "col"), None),
            P(("col", "row"), None),
            P("col", "row", None, None, None),
            P(None, "col", "row", None),
            P("col", "row"),
            P(("col", "row")),
            P(("row", "col")),
        ),
        out_specs=(P(("col", "row"), None), P(("row", "col"), None)),
        check_vma=False,
    )
```

```python
import jax
import jax.numpy as jnp
from jax import lax
from jax.experimental import pallas as pl
from jax.experimental.pallas import tpu as pltpu
from jax.sharding import PartitionSpec as P

MESH = pl.DeviceIdType.MESH
F32 = jnp.float32
BF16 = jnp.bfloat16
T = 128
SLOTS = 128
NX, NZ = 4, 8
UNROLL = 16
VMEM_LIMIT = 53 * 1024 * 1024
N_RECV = 97
N_AG = N_RS = 76


class Comm:
    def __init__(self, send_sem, recv_sems):
        self.send_sem, self.recv_sems, self.n, self.tiles = send_sem, recv_sems, 0, [0, 0]

    def slot(self):
        self.n += 1
        return self.n - 1

    def copy(self, src, dst, dev, slot, phase=0):
        return pltpu.make_async_remote_copy(
            src_ref=src,
            dst_ref=dst,
            send_sem=self.send_sem.at[phase],
            recv_sem=self.recv_sems.at[slot],
            device_id=dev,
            device_id_type=MESH,
        )

    def send(self, src, dst, dev, land=None, slot=None, phase=0):
        slot = self.slot() if slot is None else slot
        self.copy(src, dst, dev, slot, phase).start()
        self.tiles[phase] += 1
        return lambda: self.copy(src, dst if land is None else land, dev, slot).wait_recv()


def split(value):
    high = value.astype(BF16)
    return high, (value - high.astype(F32)).astype(BF16)


def kernel(
    embed_hbm, cot_hbm, rdeg_hbm, cdeg_hbm, coords_hbm, count_hbm, values,
    out_hbm,
    embed, cot, rdeg, cdeg, coords, count, table, idx,
    panel, pairs, vraw, vpair, fwd_each, bwd_each, part, from_core, ring, from_y,
    gpanel, gpair, fpart, xring, from_yh,
    out, send_sem, recv_sems, load_sems,
):
    row, col = lax.axis_index("row"), lax.axis_index("col")
    x, yh = lax.div(row, 2), lax.rem(row, 2)
    core, chip = lax.rem(col, 2), lax.div(col, 2)
    yl, z = lax.div(chip, NZ), lax.rem(chip, NZ)
    turn = 1 - 2 * core

    def zat(d):
        return lax.rem(z + turn * d + NZ, NZ)

    def xat(d):
        return lax.rem(x + turn * d + NX, NX)

    def colof(y, zz, c):
        return (y * NZ + zz) * 2 + c

    def ctile(other, d, h, c=None, sign=1):
        y = 1 - yl if other else yl
        return colof(y, zat(sign * d), core if c is None else c) * 2 + h

    def rtile(other, d, h):
        return (xat(d) * 2 + (1 - yh if other else yh)) * 2 + h

    partner = (row, col + turn)
    za = (row, colof(yl, zat(1), core))
    zb = (row, colof(yl, zat(-1), core))
    ypair = (row, colof(1 - yl, z, core))
    ypeer = (x * 2 + 1 - yh, col)
    xa = (xat(1) * 2 + yh, col)
    xb = (xat(-1) * 2 + yh, col)

    barrier = pltpu.get_barrier_semaphore()
    for dev in (za, zb, xa, xb, ypair, ypeer, partner):
        pl.semaphore_signal(barrier, inc=1, device_id=dev, device_id_type=MESH)

    inputs = []
    for n, (src, dst) in enumerate((
        (cot_hbm, cot), (rdeg_hbm, rdeg), (embed_hbm, embed), (cdeg_hbm, cdeg), (coords_hbm, coords), (count_hbm, count)
    )):
        load = pltpu.make_async_copy(src, dst, load_sems.at[n])
        load.start()
        inputs.append(load)
    loads = []
    group = SLOTS // 8
    for g in range(4):
        piece = pl.ds(g * 2 * group, 2 * group)
        load = pltpu.make_async_copy(values.at[piece], vraw.at[piece], load_sems.at[6 + g])
        load.start()
        loads.append(load)
    for load in inputs:
        load.wait()

    for h in range(2):
        half = pl.ds(h * T, T)
        rs = lax.rsqrt(rdeg[pl.ds(h, 1), :].astype(F32))
        cs = lax.rsqrt(cdeg[pl.ds(h, 1), :].astype(F32))
        gpanel[rtile(0, 0, h)] = cot[half, :].T * rs
        panel[ctile(0, 0, h)] = (embed[half, :].T * cs).T
    pl.semaphore_wait(barrier, 7)

    comm = Comm(send_sem, recv_sems)

    def share(ref, tile, dev, land):
        return comm.send(ref.at[tile], ref.at[tile], dev, ref.at[land])

    def push(src, dst, dev, slot=None):
        return comm.send(src, dst, dev, slot=slot, phase=1)

    core_slot = comm.slot()

    def col_core(tile):
        comm.send(panel.at[tile], panel.at[tile], partner, slot=core_slot)

    got_yh, xa1, xb1, xa2 = {}, {}, {}, {}

    def x_send(other, h):
        xa1[other, h] = share(gpanel, rtile(other, 0, h), xa, rtile(other, -1, h))
        xb1[other, h] = share(gpanel, rtile(other, 0, h), xb, rtile(other, 1, h))

    x_send(0, 0)
    x_send(0, 1)
    y_first = share(panel, ctile(0, 0, 0), ypair, ctile(1, 0, 0))
    got_yh[0] = share(gpanel, rtile(0, 0, 0), ypeer, rtile(1, 0, 0))
    za_got, zb_got, y_got = {}, {}, {}
    PIECES = ((0, 0), (0, 1), (1, 0))

    def z_send(p, k):
        other, h = PIECES[p]
        if k < 4:
            za_got[k + 1, p] = share(panel, ctile(other, -k, h), za, ctile(other, -k - 1, h))
        if k < 3:
            zb_got[k + 1, p] = share(panel, ctile(other, k, h), zb, ctile(other, k + 1, h))

    got_yh[1] = share(gpanel, rtile(0, 0, 1), ypeer, rtile(1, 0, 1))
    z_send(1, 0)
    z_send(0, 0)
    y_got[0] = share(panel, ctile(0, 0, 1), ypair, ctile(1, 0, 1))
    for h in range(2):
        col_core(ctile(0, 0, h))

    sub = lax.broadcasted_iota(jnp.int32, (T, T), 0)
    lane = lax.broadcasted_iota(jnp.int32, (T, T), 1)
    live = sub < count[0, 0]

    def latest(hit):
        best = jnp.max(jnp.where(hit & live, sub, -1), axis=0, keepdims=True)
        return jnp.where(best < 0, SLOTS, best)

    for n in range(2):
        key = jnp.broadcast_to(coords[pl.ds(n, 1), :], (T, T))
        down = key.T
        table[pl.ds(n, 1), :] = coords[pl.ds(n, 1), :]
        table[pl.ds(2 + n, 1), :] = latest((down == key) & (sub < lane))
        table[pl.ds(4 + n, 1), :] = latest(down == lane)
    to_smem = pltpu.make_async_copy(table, idx, load_sems.at[10])
    to_smem.start()
    fwd_each[SLOTS] = jnp.zeros((T, T), F32)
    bwd_each[SLOTS] = jnp.zeros((T, T), F32)

    def ev_row_y(h):
        def run():
            got_yh[h]()
            x_send(1, h)

        return run

    def ev_x(other, h):
        def run():
            xa1[other, h]()
            xa2[other, h] = share(gpanel, rtile(other, -1, h), xa, rtile(other, -2, h))
            xb1[other, h]()

        return run

    def ev_x_end():
        for key in ((0, 0), (0, 1), (1, 0), (1, 1)):
            xa2[key]()

    def ev_y_first():
        y_first()
        z_send(2, 0)
        col_core(ctile(1, 0, 0))

    def ev_z(k, p):
        def run():
            other, h = PIECES[p]
            za_got[k, p]()
            if k < 4:
                zb_got[k, p]()
                z_send(p, k)
            for s in (-1, 1) if k < 4 else (-1,):
                tile = ctile(other, s * k, h)
                if p == 1:
                    y_got[s * k] = share(panel, tile, ypair, ctile(1, s * k, 1))
                col_core(tile)

        return run

    def ev_y(d):
        def run():
            y_got[d]()
            col_core(ctile(1, d, 1))

        return run

    def ev_core_end():
        comm.copy(panel.at[pl.ds(0, 32)], panel.at[pl.ds(0, 32)], partner, core_slot).wait_recv()

    def do_split(g):
        def run():
            if g % 2 == 0:
                loads[g // 2].wait()

            def body(i, carry):
                for u in range(2):
                    t = g * group + i * 2 + u
                    high, low = split(vraw[t])
                    vpair[t, pl.ds(0, T), :] = high
                    vpair[t, pl.ds(T, T), :] = low
                return carry

            lax.fori_loop(0, group // 2, body, 0)

        return run

    def do_gsplit():
        to_smem.wait()

        def body(r, carry):
            high, low = split(gpanel[r])
            gpair[r, pl.ds(0, T), :] = high
            gpair[r, pl.ds(T, T), :] = low
            return carry

        lax.fori_loop(0, 4 * NX, body, 0)

    def do_bwd(g):
        def run():
            def body(i, carry):
                for u in range(UNROLL):
                    t = g * group + i * UNROLL + u
                    g2 = gpair[idx[0, t]]
                    res = jnp.dot(
                        jnp.concatenate([g2, g2], axis=1), vpair[t], preferred_element_type=F32
                    )
                    bwd_each[t] = res[:T] + res[T:] + bwd_each[idx[3, t]]
                return carry

            lax.fori_loop(0, group // UNROLL, body, 0)

        return run

    def do_ssplit():
        def body(c, carry):
            for u in range(2):
                high, low = split(panel[c * 2 + u])
                pairs[c * 2 + u, :, pl.ds(0, T)] = high
                pairs[c * 2 + u, :, pl.ds(T, T)] = low
            return carry

        lax.fori_loop(0, 4 * NZ, body, 0)

    def do_fwd(g):
        def run():
            def body(i, carry):
                for u in range(UNROLL):
                    t = g * group + i * UNROLL + u
                    s2 = pairs[idx[1, t]]
                    v2 = jnp.concatenate([vpair[t, pl.ds(0, T), :], vpair[t, pl.ds(T, T), :]], axis=1)
                    res = jnp.dot(
                        v2, jnp.concatenate([s2, s2], axis=0), preferred_element_type=F32
                    )
                    fwd_each[t] = res[:, :T] + res[:, T:] + fwd_each[idx[2, t]]
                return carry

            lax.fori_loop(0, group // UNROLL, body, 0)

        return run

    order = (4, -3, 3, -2, 2, -1, 1, 0)
    kinds = ((1, 0), (1, 1), (0, 0), (0, 1))
    core_got = {}

    def ev_pick(d):
        def run():
            n, slot = order.index(d), comm.slot()
            for m, (other, h) in enumerate(kinds):
                tile = ctile(other, d, h, 1 - core, -1)
                part[tile] = bwd_each[idx[5, tile]]
                push(part.at[tile], from_core.at[4 * n + m], partner, slot)
            four = from_core.at[pl.ds(4 * n, 4)]
            core_got[d] = (n, lambda: comm.copy(four, four, partner, slot).wait_recv())

        return run

    own_y, a_got, b_got = {}, {}, {}
    RPIECES = ((0, 0), (1, 0), (0, 1))

    def ring_send(p, d, sign, slot, got):
        other, h = RPIECES[p]
        got[p, slot] = push(
            part.at[ctile(other, d, h)], ring.at[slot * 3 + p], za if sign > 0 else zb
        )

    def ev_merge(d):
        def run():
            n, wait = core_got[d]
            wait()
            for m, (other, h) in enumerate(kinds):
                tile = ctile(other, d, h)
                part[tile] = bwd_each[idx[5, tile]] + from_core[4 * n + m]
                if (other, h) == (1, 1):
                    own_y[d] = push(part.at[tile], from_y.at[d % NZ], ypair)
                if d == 4 and h == 0:
                    ring_send(other, 4, 1, 3, a_got)
                if d == -3 and h == 0:
                    ring_send(other, -3, -1, 6, b_got)

        return run

    def ev_merge_y(d):
        def run():
            own_y[d]()
            tile = ctile(0, d, 1)
            part[tile] = part[tile] + from_y[d % NZ]
            if d == 4:
                ring_send(2, 4, 1, 3, a_got)
            if d == -3:
                ring_send(2, -3, -1, 6, b_got)

        return run

    def ev_a(p, left):
        def run():
            other, h = RPIECES[p]
            a_got[p, left]()
            tile = ctile(other, left, h)
            part[tile] = part[tile] + ring[left * 3 + p]
            if left:
                ring_send(p, left, 1, left - 1, a_got)

        return run

    def ev_b(p, left):
        def run():
            other, h = RPIECES[p]
            b_got[p, 4 + left]()
            tile = ctile(other, -left, h)
            part[tile] = part[tile] + ring[(4 + left) * 3 + p]
            if left:
                ring_send(p, -left, -1, 4 + left - 1, b_got)

        return run

    def finish(n):
        copy = pltpu.make_async_copy(out.at[n], out_hbm.at[n], load_sems.at[n])
        copy.start()
        finished.append(copy)

    def ev_grad_y():
        own_y["end"] = push(part.at[ctile(1, 0, 0)], from_y.at[NZ], ypair)

    def ev_grad(h):
        def run():
            total = part[ctile(0, 0, h)]
            if h == 0:
                own_y["end"]()
                total = total + from_y[NZ]
            cs = lax.rsqrt(cdeg[pl.ds(h, 1), :].astype(F32))
            out[2 + h] = (total * cs).T
            finish(2 + h)

        return run

    fa, fb, fy = {}, {}, {}

    def f_a2(other, h):
        fa[other, h] = push(fpart.at[rtile(other, 2, h)], xring.at[other * 2 + h], xa)

    def f_b1(other, h):
        fb[other, h] = push(fpart.at[rtile(other, -1, h)], xring.at[4 + other * 2 + h], xb)

    def ev_f_start():
        for other, d in ((1, 2), (1, -1), (0, 2), (0, -1), (1, 1), (0, 1), (1, 0), (0, 0)):
            for h in range(2):
                tile = rtile(other, d, h)
                fpart[tile] = fwd_each[idx[4, tile]]
            for h in range(2):
                if d == 2:
                    f_a2(other, h)
                if (other, d) == (1, -1):
                    f_b1(other, h)

    def ev_f_mid(other, h):
        def run():
            fa[other, h]()
            tile = rtile(other, 1, h)
            fpart[tile] = fpart[tile] + xring[other * 2 + h]
            fa[other, h] = push(fpart.at[tile], xring.at[8 + other * 2 + h], xa)
            if (other, h) == (1, 1):
                f_b1(0, 0)
                f_b1(0, 1)

        return run

    def ev_f_last(other, h):
        def run():
            fb[other, h]()
            fa[other, h]()
            tile = rtile(other, 0, h)
            fpart[tile] = fpart[tile] + (xring[4 + other * 2 + h] + xring[8 + other * 2 + h])
            if other:
                fy[h] = push(fpart.at[tile], from_yh.at[h], ypeer)

        return run

    def ev_f_end(h):
        def run():
            fy[h]()
            rs = lax.rsqrt(rdeg[pl.ds(h, 1), :].astype(F32))
            total = fpart[rtile(0, 0, h)] + from_yh[h]
            out[h] = (total.T * rs).T
            finish(h)

        return run

    finished = []

    plan = [
        ev_y_first, ev_z(1, 1), do_split(0), ev_z(1, 0), ev_row_y(0), do_split(1), ev_row_y(1), ev_z(1, 2),
        ev_x(0, 1), do_split(2), ev_x(0, 0), ev_y(0), do_split(3), do_split(4), ev_z(2, 1), ev_x(1, 0),
        ev_z(2, 0), do_split(5), ev_x(1, 1), ev_y(-1), ev_z(2, 2), ev_z(3, 1), ev_y(-2), ev_y(1), do_split(6),
        do_split(7), ev_x_end, do_gsplit, ev_z(3, 0), do_bwd(0), do_bwd(1), do_bwd(2), do_bwd(3), ev_z(3, 2),
        do_bwd(4), do_bwd(5), ev_z(4, 1), do_bwd(6), do_bwd(7), ev_pick(4), ev_pick(-3), ev_pick(3), ev_y(2),
        ev_y(3), ev_merge(4), ev_pick(-2), ev_merge(3), ev_y(-3), ev_z(4, 0), ev_merge(-3), ev_z(4, 2),
        ev_y(-4), ev_merge(-2), ev_pick(2), ev_pick(-1), ev_core_end, do_ssplit, do_fwd(0), do_fwd(1),
        ev_a(1, 3), do_fwd(2), ev_merge_y(4), do_fwd(3), do_fwd(4), ev_a(0, 3), do_fwd(5), do_fwd(6), do_fwd(7),
        ev_f_start, ev_b(1, 2), ev_merge_y(-3), ev_pick(1), ev_b(0, 2), ev_merge_y(3), ev_merge(2), ev_a(2, 3),
        ev_a(1, 2), ev_pick(0), ev_merge(-1), ev_a(0, 2), ev_merge(1), ev_f_mid(1, 0), ev_merge(0),
        ev_merge_y(-2), ev_b(2, 2), ev_b(1, 1), ev_f_mid(1, 1), ev_merge_y(2), ev_merge_y(-1), ev_a(2, 2),
        ev_f_mid(0, 1), ev_a(1, 1), ev_f_last(1, 0), ev_merge_y(1), ev_a(0, 1), ev_f_last(1, 1), ev_b(2, 1),
        ev_b(1, 0), ev_merge_y(0), ev_a(2, 1), ev_f_mid(0, 0), ev_b(0, 1), ev_a(1, 0), ev_grad_y, ev_a(2, 0),
        ev_a(0, 0), ev_f_last(0, 0), ev_f_last(0, 1), ev_b(2, 0), ev_grad(1), ev_f_end(0), ev_f_end(1),
        ev_b(0, 0), ev_grad(0),
    ]
    for step in plan:
        step()
    for copy in finished:
        copy.wait()
    assert comm.tiles == [N_AG, N_RS] and comm.n == N_RECV, (comm.tiles, comm.n)
    for phase, n in ((0, N_AG), (1, N_RS)):
        comm.copy(fwd_each.at[pl.ds(0, n)], fwd_each.at[pl.ds(0, n)], partner, 0, phase).wait_send()


def per_device(embed, cotangent, tile_values, tile_coords, tile_count, row_degree, col_degree):
    anywhere = pl.BlockSpec(memory_space=pl.ANY)
    hbm = lambda a: pltpu.with_memory_space_constraint(a, pltpu.HBM)
    tile = lambda n, dtype=F32, a=T, b=T: pltpu.VMEM((n, a, b), dtype)
    ints = lambda n: pltpu.VMEM((n, T), jnp.int32)
    out = pl.pallas_call(
        kernel,
        out_shape=jax.ShapeDtypeStruct((4, T, T), F32),
        in_specs=[anywhere] * 7,
        out_specs=anywhere,
        scratch_shapes=[
            pltpu.VMEM((2 * T, T), F32), pltpu.VMEM((2 * T, T), F32), ints(2), ints(2), ints(2),
            pltpu.SMEM((1, 1), jnp.int32), ints(8), pltpu.SMEM((8, T), jnp.int32),
            tile(64), tile(64, BF16, T, 2 * T), tile(SLOTS), tile(SLOTS, BF16, 2 * T, T),
            tile(SLOTS + 1), tile(SLOTS + 1), tile(64), tile(32), tile(21), tile(9),
            tile(16), tile(16, BF16, 2 * T, T), tile(16), tile(12), tile(2),
            tile(4),
            pltpu.SemaphoreType.DMA((2,)),
            pltpu.SemaphoreType.DMA((N_RECV,)),
            pltpu.SemaphoreType.DMA((11,)),
        ],
        compiler_params=pltpu.CompilerParams(
            collective_id=0, has_side_effects=True, vmem_limit_bytes=VMEM_LIMIT
        ),
    )(
        hbm(embed), hbm(cotangent), hbm(row_degree.reshape(2, T)), hbm(col_degree.reshape(2, T)),
        hbm(tile_coords.reshape(2, T)), tile_count, hbm(tile_values[0, 0]),
    )
    return out[:2].reshape(2 * T, T), out[2:].reshape(2 * T, T)


def solution(mesh):
    return jax.shard_map(
        per_device,
        mesh=mesh,
        in_specs=(
            P(("row", "col"), None),
            P(("col", "row"), None),
            P("col", "row", None, None, None),
            P(None, "col", "row", None),
            P("col", "row"),
            P(("col", "row")),
            P(("row", "col")),
        ),
        out_specs=(P(("col", "row"), None), P(("row", "col"), None)),
        check_vma=False,
    )
```

```python
import jax
import jax.numpy as jnp
from jax import lax
from jax.experimental import pallas as pl
from jax.experimental.pallas import tpu as pltpu
from jax.sharding import PartitionSpec as P

MESH = pl.DeviceIdType.MESH
F32 = jnp.float32
BF16 = jnp.bfloat16
T = 128
SLOTS = 128
NX, NZ = 4, 8
UNROLL = 16
VMEM_LIMIT = 53 * 1024 * 1024
N_RECV = 97
N_AG = N_RS = 76


class Comm:
    def __init__(self, send_sem, recv_sems):
        self.send_sem, self.recv_sems, self.n, self.tiles = send_sem, recv_sems, 0, [0, 0]

    def slot(self):
        self.n += 1
        return self.n - 1

    def copy(self, src, dst, dev, slot, phase=0):
        return pltpu.make_async_remote_copy(
            src_ref=src,
            dst_ref=dst,
            send_sem=self.send_sem.at[phase],
            recv_sem=self.recv_sems.at[slot],
            device_id=dev,
            device_id_type=MESH,
        )

    def send(self, src, dst, dev, land=None, slot=None, phase=0):
        slot = self.slot() if slot is None else slot
        self.copy(src, dst, dev, slot, phase).start()
        self.tiles[phase] += 1
        return lambda: self.copy(src, dst if land is None else land, dev, slot).wait_recv()


def split(value):
    high = value.astype(BF16)
    return high, (value - high.astype(F32)).astype(BF16)


def kernel(
    embed_hbm, cot_hbm, rdeg_hbm, cdeg_hbm, coords_hbm, count_hbm, values,
    out_hbm,
    embed, cot, rdeg, cdeg, coords, count, table, idx,
    panel, pairs, vraw, vpair, fwd_each, bwd_each, part, from_core, ring, from_y,
    gpanel, gpair, fpart, xring, from_yh,
    out, send_sem, recv_sems, load_sems,
):
    row, col = lax.axis_index("row"), lax.axis_index("col")
    x, yh = lax.div(row, 2), lax.rem(row, 2)
    core, chip = lax.rem(col, 2), lax.div(col, 2)
    yl, z = lax.div(chip, NZ), lax.rem(chip, NZ)
    turn = 1 - 2 * core

    def zat(d):
        return lax.rem(z + turn * d + NZ, NZ)

    def xat(d):
        return lax.rem(x + turn * d + NX, NX)

    def colof(y, zz, c):
        return (y * NZ + zz) * 2 + c

    def ctile(other, d, h, c=None, sign=1):
        y = 1 - yl if other else yl
        return colof(y, zat(sign * d), core if c is None else c) * 2 + h

    def rtile(other, d, h):
        return (xat(d) * 2 + (1 - yh if other else yh)) * 2 + h

    partner = (row, col + turn)
    za = (row, colof(yl, zat(1), core))
    zb = (row, colof(yl, zat(-1), core))
    ypair = (row, colof(1 - yl, z, core))
    ypeer = (x * 2 + 1 - yh, col)
    xa = (xat(1) * 2 + yh, col)
    xb = (xat(-1) * 2 + yh, col)

    barrier = pltpu.get_barrier_semaphore()
    for dev in (za, zb, xa, xb, ypair, ypeer, partner):
        pl.semaphore_signal(barrier, inc=1, device_id=dev, device_id_type=MESH)

    inputs = []
    for n, (src, dst) in enumerate((
        (cot_hbm, cot), (rdeg_hbm, rdeg), (embed_hbm, embed), (cdeg_hbm, cdeg), (coords_hbm, coords), (count_hbm, count)
    )):
        load = pltpu.make_async_copy(src, dst, load_sems.at[n])
        load.start()
        inputs.append(load)
    loads = []
    group = SLOTS // 8
    for g in range(4):
        piece = pl.ds(g * 2 * group, 2 * group)
        load = pltpu.make_async_copy(values.at[piece], vraw.at[piece], load_sems.at[6 + g])
        load.start()
        loads.append(load)
    for load in inputs:
        load.wait()

    for h in range(2):
        half = pl.ds(h * T, T)
        rs = lax.rsqrt(rdeg[pl.ds(h, 1), :].astype(F32))
        cs = lax.rsqrt(cdeg[pl.ds(h, 1), :].astype(F32))
        gpanel[rtile(0, 0, h)] = cot[half, :].T * rs
        panel[ctile(0, 0, h)] = (embed[half, :].T * cs).T
    pl.semaphore_wait(barrier, 7)

    comm = Comm(send_sem, recv_sems)

    def share(ref, tile, dev, land):
        return comm.send(ref.at[tile], ref.at[tile], dev, ref.at[land])

    def push(src, dst, dev, slot=None):
        return comm.send(src, dst, dev, slot=slot, phase=1)

    core_slot = comm.slot()

    def col_core(tile):
        comm.send(panel.at[tile], panel.at[tile], partner, slot=core_slot)

    got_yh, xa1, xb1, xa2 = {}, {}, {}, {}

    def x_send(other, h):
        xa1[other, h] = share(gpanel, rtile(other, 0, h), xa, rtile(other, -1, h))
        xb1[other, h] = share(gpanel, rtile(other, 0, h), xb, rtile(other, 1, h))

    x_send(0, 0)
    x_send(0, 1)
    y_first = share(panel, ctile(0, 0, 0), ypair, ctile(1, 0, 0))
    got_yh[0] = share(gpanel, rtile(0, 0, 0), ypeer, rtile(1, 0, 0))
    za_got, zb_got, y_got = {}, {}, {}
    PIECES = ((0, 0), (0, 1), (1, 0))

    def z_send(p, k):
        other, h = PIECES[p]
        if k < 4:
            za_got[k + 1, p] = share(panel, ctile(other, -k, h), za, ctile(other, -k - 1, h))
        if k < 3:
            zb_got[k + 1, p] = share(panel, ctile(other, k, h), zb, ctile(other, k + 1, h))

    got_yh[1] = share(gpanel, rtile(0, 0, 1), ypeer, rtile(1, 0, 1))
    z_send(1, 0)
    z_send(0, 0)
    y_got[0] = share(panel, ctile(0, 0, 1), ypair, ctile(1, 0, 1))
    for h in range(2):
        col_core(ctile(0, 0, h))

    sub = lax.broadcasted_iota(jnp.int32, (T, T), 0)
    lane = lax.broadcasted_iota(jnp.int32, (T, T), 1)
    live = sub < count[0, 0]

    def latest(hit):
        best = jnp.max(jnp.where(hit & live, sub, -1), axis=0, keepdims=True)
        return jnp.where(best < 0, SLOTS, best)

    for n in range(2):
        key = jnp.broadcast_to(coords[pl.ds(n, 1), :], (T, T))
        down = key.T
        table[pl.ds(n, 1), :] = coords[pl.ds(n, 1), :]
        table[pl.ds(2 + n, 1), :] = latest((down == key) & (sub < lane))
        table[pl.ds(4 + n, 1), :] = latest(down == lane)
    to_smem = pltpu.make_async_copy(table, idx, load_sems.at[10])
    to_smem.start()
    fwd_each[SLOTS] = jnp.zeros((T, T), F32)
    bwd_each[SLOTS] = jnp.zeros((T, T), F32)

    def ev_row_y(h):
        def run():
            got_yh[h]()
            x_send(1, h)

        return run

    def ev_x(other, h):
        def run():
            xa1[other, h]()
            xa2[other, h] = share(gpanel, rtile(other, -1, h), xa, rtile(other, -2, h))
            xb1[other, h]()

        return run

    def ev_x_end():
        for key in ((0, 0), (0, 1), (1, 0), (1, 1)):
            xa2[key]()

    def ev_y_first():
        y_first()
        z_send(2, 0)
        col_core(ctile(1, 0, 0))

    def ev_z(k, p):
        def run():
            other, h = PIECES[p]
            za_got[k, p]()
            if k < 4:
                zb_got[k, p]()
                z_send(p, k)
            for s in (-1, 1) if k < 4 else (-1,):
                tile = ctile(other, s * k, h)
                if p == 1:
                    y_got[s * k] = share(panel, tile, ypair, ctile(1, s * k, 1))
                col_core(tile)

        return run

    def ev_y(d):
        def run():
            y_got[d]()
            col_core(ctile(1, d, 1))

        return run

    def ev_core_end():
        comm.copy(panel.at[pl.ds(0, 32)], panel.at[pl.ds(0, 32)], partner, core_slot).wait_recv()

    def do_split(g):
        def run():
            if g % 2 == 0:
                loads[g // 2].wait()

            def body(i, carry):
                for u in range(2):
                    t = g * group + i * 2 + u
                    high, low = split(vraw[t])
                    vpair[t, pl.ds(0, T), :] = high
                    vpair[t, pl.ds(T, T), :] = low
                return carry

            lax.fori_loop(0, group // 2, body, 0)

        return run

    def do_gsplit():
        to_smem.wait()

        def body(r, carry):
            high, low = split(gpanel[r])
            gpair[r, pl.ds(0, T), :] = high
            gpair[r, pl.ds(T, T), :] = low
            return carry

        lax.fori_loop(0, 4 * NX, body, 0)

    def do_bwd(g):
        def run():
            def body(i, carry):
                for u in range(UNROLL):
                    t = g * group + i * UNROLL + u
                    g2 = gpair[idx[0, t]]
                    res = jnp.dot(
                        jnp.concatenate([g2, g2], axis=1), vpair[t], preferred_element_type=F32
                    )
                    bwd_each[t] = res[:T] + res[T:] + bwd_each[idx[3, t]]
                return carry

            lax.fori_loop(0, group // UNROLL, body, 0)

        return run

    def do_ssplit():
        def body(c, carry):
            for u in range(2):
                high, low = split(panel[c * 2 + u])
                pairs[c * 2 + u, :, pl.ds(0, T)] = high
                pairs[c * 2 + u, :, pl.ds(T, T)] = low
            return carry

        lax.fori_loop(0, 4 * NZ, body, 0)

    def do_fwd(g):
        def run():
            def body(i, carry):
                for u in range(UNROLL):
                    t = g * group + i * UNROLL + u
                    s2 = pairs[idx[1, t]]
                    v2 = jnp.concatenate([vpair[t, pl.ds(0, T), :], vpair[t, pl.ds(T, T), :]], axis=1)
                    res = jnp.dot(
                        v2, jnp.concatenate([s2, s2], axis=0), preferred_element_type=F32
                    )
                    fwd_each[t] = res[:, :T] + res[:, T:] + fwd_each[idx[2, t]]
                return carry

            lax.fori_loop(0, group // UNROLL, body, 0)

        return run

    order = (4, -3, 3, -2, 2, -1, 1, 0)
    kinds = ((1, 0), (1, 1), (0, 0), (0, 1))
    core_got = {}

    def ev_pick(d):
        def run():
            n, slot = order.index(d), comm.slot()
            for m, (other, h) in enumerate(kinds):
                tile = ctile(other, d, h, 1 - core, -1)
                part[tile] = bwd_each[idx[5, tile]]
                push(part.at[tile], from_core.at[4 * n + m], partner, slot)
            four = from_core.at[pl.ds(4 * n, 4)]
            core_got[d] = (n, lambda: comm.copy(four, four, partner, slot).wait_recv())

        return run

    own_y, a_got, b_got = {}, {}, {}
    RPIECES = ((0, 0), (1, 0), (0, 1))

    def ring_send(p, d, sign, slot, got):
        other, h = RPIECES[p]
        got[p, slot] = push(
            part.at[ctile(other, d, h)], ring.at[slot * 3 + p], za if sign > 0 else zb
        )

    def ev_merge(d):
        def run():
            n, wait = core_got[d]
            wait()
            for m, (other, h) in enumerate(kinds):
                tile = ctile(other, d, h)
                part[tile] = bwd_each[idx[5, tile]] + from_core[4 * n + m]
                if (other, h) == (1, 1):
                    own_y[d] = push(part.at[tile], from_y.at[d % NZ], ypair)
                if d == 4 and h == 0:
                    ring_send(other, 4, 1, 3, a_got)
                if d == -3 and h == 0:
                    ring_send(other, -3, -1, 6, b_got)

        return run

    def ev_merge_y(d):
        def run():
            own_y[d]()
            tile = ctile(0, d, 1)
            part[tile] = part[tile] + from_y[d % NZ]
            if d == 4:
                ring_send(2, 4, 1, 3, a_got)
            if d == -3:
                ring_send(2, -3, -1, 6, b_got)

        return run

    def ev_a(p, left):
        def run():
            other, h = RPIECES[p]
            a_got[p, left]()
            tile = ctile(other, left, h)
            part[tile] = part[tile] + ring[left * 3 + p]
            if left:
                ring_send(p, left, 1, left - 1, a_got)

        return run

    def ev_b(p, left):
        def run():
            other, h = RPIECES[p]
            b_got[p, 4 + left]()
            tile = ctile(other, -left, h)
            part[tile] = part[tile] + ring[(4 + left) * 3 + p]
            if left:
                ring_send(p, -left, -1, 4 + left - 1, b_got)

        return run

    def finish(n):
        copy = pltpu.make_async_copy(out.at[n], out_hbm.at[n], load_sems.at[n])
        copy.start()
        finished.append(copy)

    def ev_grad_y():
        own_y["end"] = push(part.at[ctile(1, 0, 0)], from_y.at[NZ], ypair)

    def ev_grad(h):
        def run():
            total = part[ctile(0, 0, h)]
            if h == 0:
                own_y["end"]()
                total = total + from_y[NZ]
            cs = lax.rsqrt(cdeg[pl.ds(h, 1), :].astype(F32))
            out[2 + h] = (total * cs).T
            finish(2 + h)

        return run

    fa, fb, fy = {}, {}, {}

    def f_a2(other, h):
        fa[other, h] = push(fpart.at[rtile(other, 2, h)], xring.at[other * 2 + h], xa)

    def f_b1(other, h):
        fb[other, h] = push(fpart.at[rtile(other, -1, h)], xring.at[4 + other * 2 + h], xb)

    def ev_f_start():
        for other, d in ((1, 2), (1, -1), (0, 2), (0, -1), (1, 1), (0, 1), (1, 0), (0, 0)):
            for h in range(2):
                tile = rtile(other, d, h)
                fpart[tile] = fwd_each[idx[4, tile]]
            for h in range(2):
                if d == 2:
                    f_a2(other, h)
                if (other, d) == (1, -1):
                    f_b1(other, h)

    def ev_f_mid(other, h):
        def run():
            fa[other, h]()
            tile = rtile(other, 1, h)
            fpart[tile] = fpart[tile] + xring[other * 2 + h]
            fa[other, h] = push(fpart.at[tile], xring.at[8 + other * 2 + h], xa)
            if (other, h) == (1, 1):
                f_b1(0, 0)
                f_b1(0, 1)

        return run

    def ev_f_last(other, h):
        def run():
            fb[other, h]()
            fa[other, h]()
            tile = rtile(other, 0, h)
            fpart[tile] = fpart[tile] + (xring[4 + other * 2 + h] + xring[8 + other * 2 + h])
            if other:
                fy[h] = push(fpart.at[tile], from_yh.at[h], ypeer)

        return run

    def ev_f_end(h):
        def run():
            fy[h]()
            rs = lax.rsqrt(rdeg[pl.ds(h, 1), :].astype(F32))
            total = fpart[rtile(0, 0, h)] + from_yh[h]
            out[h] = (total.T * rs).T
            finish(h)

        return run

    finished = []

    plan = [
        ev_y_first, do_split(0), ev_z(1, 1), do_split(1), ev_x(0, 1), do_split(2), ev_z(1, 0), ev_row_y(0),
        ev_row_y(1), do_split(3), ev_z(1, 2), do_split(4), ev_z(2, 1), do_split(5), ev_x(0, 0), ev_x(1, 0),
        do_split(6), ev_z(2, 0), ev_x(1, 1), ev_z(2, 2), ev_y(-2), ev_y(2), ev_y(-1), do_split(7), ev_y(0),
        ev_z(3, 1), ev_x_end, do_gsplit, do_bwd(0), do_bwd(1), do_bwd(2), ev_z(3, 0), do_bwd(3), do_bwd(4),
        do_bwd(5), ev_z(3, 2), do_bwd(6), do_bwd(7), ev_z(4, 1), ev_y(1), ev_pick(4), ev_y(-3), ev_pick(-3),
        ev_y(3), ev_pick(3), ev_merge(4), ev_z(4, 2), ev_merge(-3), ev_pick(-2), ev_z(4, 0), ev_y(-4),
        ev_pick(2), ev_pick(-1), ev_pick(1), ev_merge(3), ev_merge(-2), ev_core_end, do_ssplit, ev_a(1, 3),
        do_fwd(0), do_fwd(1), ev_merge_y(4), do_fwd(2), do_fwd(3), do_fwd(4), ev_a(0, 3), do_fwd(5), ev_b(1, 2),
        do_fwd(6), do_fwd(7), ev_f_start, ev_merge(2), ev_merge(1), ev_a(1, 2), ev_merge_y(3), ev_a(2, 3),
        ev_pick(0), ev_merge_y(-3), ev_b(0, 2), ev_a(0, 2), ev_merge(-1), ev_merge_y(-2), ev_merge_y(2),
        ev_f_mid(1, 0), ev_b(1, 1), ev_a(2, 2), ev_f_mid(1, 1), ev_merge(0), ev_b(2, 2), ev_a(1, 1),
        ev_f_last(1, 0), ev_f_mid(0, 1), ev_b(0, 1), ev_merge_y(-1), ev_f_last(1, 1), ev_merge_y(1),
        ev_merge_y(0), ev_a(2, 1), ev_b(2, 1), ev_b(1, 0), ev_f_mid(0, 0), ev_a(1, 0), ev_a(0, 1), ev_grad_y,
        ev_a(2, 0), ev_f_last(0, 1), ev_b(0, 0), ev_f_last(0, 0), ev_b(2, 0), ev_f_end(0), ev_grad(1),
        ev_a(0, 0), ev_f_end(1), ev_grad(0),
    ]
    for step in plan:
        step()
    for copy in finished:
        copy.wait()
    assert comm.tiles == [N_AG, N_RS] and comm.n == N_RECV, (comm.tiles, comm.n)
    for phase, n in ((0, N_AG), (1, N_RS)):
        comm.copy(fwd_each.at[pl.ds(0, n)], fwd_each.at[pl.ds(0, n)], partner, 0, phase).wait_send()


def per_device(embed, cotangent, tile_values, tile_coords, tile_count, row_degree, col_degree):
    anywhere = pl.BlockSpec(memory_space=pl.ANY)
    hbm = lambda a: pltpu.with_memory_space_constraint(a, pltpu.HBM)
    tile = lambda n, dtype=F32, a=T, b=T: pltpu.VMEM((n, a, b), dtype)
    ints = lambda n: pltpu.VMEM((n, T), jnp.int32)
    out = pl.pallas_call(
        kernel,
        out_shape=jax.ShapeDtypeStruct((4, T, T), F32),
        in_specs=[anywhere] * 7,
        out_specs=anywhere,
        scratch_shapes=[
            pltpu.VMEM((2 * T, T), F32), pltpu.VMEM((2 * T, T), F32), ints(2), ints(2), ints(2),
            pltpu.SMEM((1, 1), jnp.int32), ints(8), pltpu.SMEM((8, T), jnp.int32),
            tile(64), tile(64, BF16, T, 2 * T), tile(SLOTS), tile(SLOTS, BF16, 2 * T, T),
            tile(SLOTS + 1), tile(SLOTS + 1), tile(64), tile(32), tile(21), tile(9),
            tile(16), tile(16, BF16, 2 * T, T), tile(16), tile(12), tile(2),
            tile(4),
            pltpu.SemaphoreType.DMA((2,)),
            pltpu.SemaphoreType.DMA((N_RECV,)),
            pltpu.SemaphoreType.DMA((11,)),
        ],
        compiler_params=pltpu.CompilerParams(
            collective_id=0, has_side_effects=True, vmem_limit_bytes=VMEM_LIMIT
        ),
    )(
        hbm(embed), hbm(cotangent), hbm(row_degree.reshape(2, T)), hbm(col_degree.reshape(2, T)),
        hbm(tile_coords.reshape(2, T)), tile_count, hbm(tile_values[0, 0]),
    )
    return out[:2].reshape(2 * T, T), out[2:].reshape(2 * T, T)


def solution(mesh):
    return jax.shard_map(
        per_device,
        mesh=mesh,
        in_specs=(
            P(("row", "col"), None),
            P(("col", "row"), None),
            P("col", "row", None, None, None),
            P(None, "col", "row", None),
            P("col", "row"),
            P(("col", "row")),
            P(("row", "col")),
        ),
        out_specs=(P(("col", "row"), None), P(("row", "col"), None)),
        check_vma=False,
    )
```
